256 devices in a mesh: seq: 128 (over y, x, z), head: 2 (over core).
Axes of the slice: x: 4, y: 4, z: 8, core: 2. Of those that a mesh axis runs over, the one named last changes fastest.
Arguments:
- query_rows: bfloat16 [49152, 2048], P('seq', 'head'), may hold values from -41 to 41
- key_rows: bfloat16 [49152, 2048], P('seq', 'head'), may hold values from -4 to 4, as said below
- value_rows: bfloat16 [49152, 2048], P('seq', 'head'), may hold values from -6 to 6
- out_grad: bfloat16 [49152, 2048], P('seq'), may hold values from -6 to 6
- cluster_ids: int32 [16, 49152, 1], P('head', 'seq'), may hold values from 0 to 255; in each aligned block of 384 rows (0 to 383, 384 to 767, ..., all dimensions but the last counted through in order) at most 2 rows name the same one
- out_weight: bfloat16 [2048, 2048], P('head'), may hold values from -0.125 to 0.125
Outputs:
- layer_out: bfloat16 [49152, 2048], P('seq', 'head')
- query_grad: bfloat16 [49152, 2048], P('seq', 'head')
- key_grad: bfloat16 [49152, 2048], P('seq', 'head')
- value_grad: bfloat16 [49152, 2048], P('seq', 'head')
The draws below stay inside these ranges and needn't reach their ends.
Inputs may be any that keep to these rules, and one draw needn't show every extreme that they name: `cluster_ids`: in each head the 384 tokens of one index of seq (aligned blocks of the token dimension) name no cluster more than 2 times, a bound that some block reaches in every draw. `key_rows`: no token's key in any head is all zeros.
All inputs are finite; a program needn't handle non-finite values.
Results may differ from the reference program's by a relative error of at most 0.009.
Values may be sent and summed in bfloat16 or wider, within the bound.
No kernel may reach another device: no remote copies, remote signals or barrier semaphores. Data moves between devices by JAX's collectives and lax.ppermute only.
A program may use at most 128 MiB of HBM per device.

```python
import math
import jax
import jax.numpy as jnp
import numpy as np
from jax import lax

HEADS = 16
DH = 128
D = 2048
CLUSTERS = 256
TOK_DEV = 384
MOST = 2
SLOTS = 256
TOKENS = 49152
N_SEQ = 128


def key_field(key):
    inner = jax.random.fold_in(key, 11)
    field = jnp.clip(jax.random.normal(inner, (TOKENS, HEADS * DH), jnp.float32), -4.0, 4.0)
    return field.astype(jnp.bfloat16).astype(jnp.float32)


def draw_key_rows(key, part):
    return key_field(key).astype(jnp.bfloat16)


def draw_query_rows(key, part):
    drawn = jnp.clip(jax.random.normal(jax.random.fold_in(key, 23), (TOKENS, HEADS * DH), jnp.float32), -4.0, 4.0)
    return drawn.astype(jnp.bfloat16)


def block_scale(stream_key, dims, cuts, low, largest):
    level = 1.0
    for position, parts in cuts:
        steps = jax.random.uniform(jax.random.fold_in(jax.random.fold_in(stream_key, 6), position), (parts,), jnp.float32, low / len(cuts), largest / len(cuts))
        level = level * jnp.repeat(jnp.exp(steps), dims[position] // parts).reshape((-1,) + (1,) * (len(dims) - 1 - position))
    return level


def routed_block(key, own, number, rows, number_of, top, most, skew):
    sequence = jax.random.permutation(key, number_of)
    packed, ordinary = shares(number_of, rows * top, most, skew, True), shares(number_of, rows * top, most, skew, False)
    places = jnp.arange(number_of)

    def named(sizes, offset_by):
        used = int((sizes > 0).sum())
        fixed = max(1, used // 4)
        passed = fixed + (places - fixed + offset_by * (used - fixed)) % max(1, number_of - fixed)
        return jnp.zeros((number_of,), jnp.int32).at[sequence[jnp.where(places < fixed, places, passed)]].set(jnp.asarray(sizes, jnp.int32))

    sizes = jnp.where(number % 4 == 0, named(packed, number // 4), named(ordinary, number - number // 4 - 1))
    mixed = jax.random.permutation(jax.random.fold_in(own, 3), number_of)
    source_of, sink = mixed[0:number_of // 2 * 2:2], mixed[1:number_of // 2 * 2:2]
    room = jnp.minimum(sizes[source_of] - 1, most - sizes[sink]) // 2
    room = jnp.where((source_of == sequence[0]) | (sink == sequence[0]) | (sizes[sink] == 0), 0, jnp.maximum(room, 0))
    passed = jax.random.randint(jax.random.fold_in(own, 4), (number_of // 2,), 0, 1 << 20) % (room + 1)
    sizes = sizes.at[source_of].add(-passed).at[sink].add(passed)
    labels = jnp.searchsorted(jnp.cumsum(sizes), jnp.arange(rows * top), side="right").astype(jnp.int32)
    table = labels.reshape(top, rows).T
    table = table[jax.random.permutation(jax.random.fold_in(own, 1), rows)]
    offset_by = jax.random.randint(jax.random.fold_in(own, 2), (rows, 1), 0, top)
    return jnp.take_along_axis(table, (jnp.arange(top)[None, :] + offset_by) % top, axis=1)


def shares(amount, total, reach, lean, full):
    loads = [(1 << 20) // math.isqrt(standing ** lean) + 1 for standing in range(1, amount + 1)]
    largest = reach if full else min(reach, max(-(-total // amount), total * loads[0] // sum(loads)))
    least = 1 if total - largest >= amount - 1 else 0
    counts, surplus = [largest] + [least] * (amount - 1), total - largest - least * (amount - 1)
    while surplus > 0:
        movable = [i for i in range(1, amount) if counts[i] < largest] or [i for i in range(1, amount) if counts[i] < reach]
        whole, budget = sum([loads[i] for i in movable]), surplus
        for i in movable:
            addition = min(reach - counts[i], max(1, budget * loads[i] // whole), surplus)
            counts[i] = counts[i] + addition
            surplus = surplus - addition
    return np.array(counts)


def noise(rng, dims, scale, most, cuts=(), held_as=jnp.bfloat16):
    gain = block_scale(rng, dims, cuts, -0.22, 0.18) if cuts else 1.0
    drawn = jax.random.normal(rng, dims, jnp.float32) * scale * gain
    return jnp.minimum(jnp.maximum(drawn, -most), most).astype(held_as)


def setup_inputs(seed: int = 0) -> dict:
    arg_keys = jax.random.split(jax.random.key(seed), 7)
    query_rows = draw_query_rows(jax.random.fold_in(arg_keys[6], 71), 0)
    key_rows = draw_key_rows(jax.random.fold_in(arg_keys[6], 71), 0)
    value_rows = noise(arg_keys[2], (TOKENS, HEADS * DH), 1.0, 6.0, ((0, 128), (1, 2)))
    out_grad = noise(arg_keys[3], (TOKENS, D), 1.0, 6.0, ((0, 128),))
    cluster_ids_keys = jax.random.split(jax.random.fold_in(arg_keys[4], 1), HEADS * TOKENS // TOK_DEV)
    cluster_ids_turns = jax.random.permutation(jax.random.fold_in(arg_keys[4], 3), HEADS * TOKENS // TOK_DEV)
    cluster_ids = jax.vmap(lambda own, number: routed_block(jax.random.fold_in(arg_keys[4], 2), own, number, TOK_DEV, CLUSTERS, 1, MOST, 2))(cluster_ids_keys, cluster_ids_turns).reshape((HEADS, TOKENS, 1))
    out_weight = noise(arg_keys[5], (HEADS * DH, D), (HEADS * DH) ** -0.5, 0.125, ((0, 2),))
    return dict(query_rows=query_rows, key_rows=key_rows, value_rows=value_rows, out_grad=out_grad, cluster_ids=cluster_ids, out_weight=out_weight)


NEGATIVE = -1.0e30


def slot_rows(cluster, per_cluster):
    count = cluster.shape[1]
    matches = cluster[:, :, None] == cluster[:, None, :]
    order_ids = jnp.arange(count, dtype=jnp.int32)
    earlier = order_ids[:, None] > order_ids[None, :]
    before = jnp.sum(jnp.logical_and(matches, earlier[None]).astype(jnp.int32), axis=2)
    return (cluster * per_cluster + before).astype(jnp.int32)


def cluster_attention(query_slots, key_slots, value_slots, grad_slots, occupied):
    scale = DH ** -0.5
    qf = query_slots.astype(jnp.float32)
    kf = key_slots.astype(jnp.float32)
    vf = value_slots.astype(jnp.float32)
    gf = grad_slots.astype(jnp.float32)
    scores = jnp.einsum("cqd,ckd->cqk", qf, kf) * scale
    order_ids = jnp.arange(query_slots.shape[1], dtype=jnp.int32)
    causal = order_ids[None, :] <= order_ids[:, None]
    allowed = jnp.logical_and(causal[None], occupied[:, None, :] > 0)
    scores = jnp.where(allowed, scores, NEGATIVE)
    row_max = jnp.max(scores, axis=2, keepdims=True)
    weights = jnp.exp(scores - row_max)
    probs_full = weights / jnp.sum(weights, axis=2, keepdims=True)
    probs_half = probs_full.astype(jnp.bfloat16)
    probs_back = probs_half.astype(jnp.float32)
    attn_out = jnp.einsum("cqk,ckd->cqd", probs_back, vf).astype(jnp.bfloat16)
    dprob = jnp.einsum("cqd,ckd->cqk", gf, vf)
    delta = jnp.sum(probs_full * dprob, axis=2, keepdims=True)
    dscore = (probs_full * (dprob - delta)).astype(jnp.bfloat16).astype(jnp.float32)
    query_grad = (jnp.einsum("cqk,ckd->cqd", dscore, kf) * scale).astype(jnp.bfloat16)
    key_grad = (jnp.einsum("cqk,cqd->ckd", dscore, qf) * scale).astype(jnp.bfloat16)
    value_grad = jnp.einsum("cqk,cqd->ckd", probs_back, gf).astype(jnp.bfloat16)
    return attn_out, query_grad, key_grad, value_grad


def reference(query_rows, key_rows, value_rows, out_grad, cluster_ids, out_weight):
    attn_grad = jnp.dot(out_grad, out_weight.T, preferred_element_type=jnp.float32).astype(jnp.bfloat16)

    def one_head(head_id):
        start = (head_id * DH).astype(jnp.int32)
        cluster = lax.dynamic_index_in_dim(cluster_ids, head_id, 0, keepdims=False)[:, 0]
        blocks = cluster.reshape(N_SEQ, TOK_DEV)
        source = jnp.arange(N_SEQ, dtype=jnp.int32)[:, None]
        slot_index = (slot_rows(blocks, SLOTS) + source * MOST).reshape(TOKENS).astype(jnp.int32)

        def to_slots(whole):
            rows = lax.dynamic_slice_in_dim(whole, start, DH, 1)
            table = jnp.zeros((CLUSTERS * SLOTS, DH), jnp.bfloat16).at[slot_index].set(rows)
            return table.reshape(CLUSTERS, SLOTS, DH)

        occupied = jnp.zeros((CLUSTERS * SLOTS,), jnp.bfloat16).at[slot_index].set(1.0).reshape(CLUSTERS, SLOTS)
        results = cluster_attention(to_slots(query_rows), to_slots(key_rows), to_slots(value_rows), to_slots(attn_grad), occupied)
        return tuple(item.reshape(CLUSTERS * SLOTS, DH)[slot_index] for item in results)

    attn_heads, query_heads, key_heads, value_heads = lax.map(one_head, jnp.arange(HEADS, dtype=jnp.int32))

    def to_tokens(stacked):
        return jnp.transpose(stacked, (1, 0, 2)).reshape(TOKENS, HEADS * DH)

    attn = to_tokens(attn_heads)
    layer_out = jnp.dot(attn, out_weight, preferred_element_type=jnp.float32).astype(jnp.bfloat16)
    return layer_out, to_tokens(query_heads), to_tokens(key_heads), to_tokens(value_heads)
```

```python
import functools

import jax
import jax.numpy as jnp
from jax import lax
from jax.experimental import pallas as pl
from jax.experimental.pallas import tpu as pltpu
from jax.sharding import PartitionSpec as P

CLUSTERS = 256
MOST = 2
DH = 128
SEQ = 128
HEADS = 8
TOK = 384
PER_HEAD = CLUSTERS * MOST
OWNERS = SEQ // HEADS
ROWS = PER_HEAD // OWNERS
OWNED = ROWS // MOST
SLOTS = SEQ * MOST
GROUP = 8
EMPTY = 64.0
NEGATIVE = -1e30
SCALE = DH ** -0.5
F32 = jnp.float32
BF16 = jnp.bfloat16


def slot_of_row(ids_row, ids_col):
    u = lax.broadcasted_iota(jnp.int32, (TOK, TOK), 0)
    t = lax.broadcasted_iota(jnp.int32, (TOK, TOK), 1)
    same = jnp.logical_and(ids_col == ids_row, u < t)
    before = jnp.max(jnp.where(same, 1, 0), axis=0, keepdims=True)
    return ids_row * MOST + before


def slot_of_col(ids_row, ids_col):
    t = lax.broadcasted_iota(jnp.int32, (TOK, TOK), 0)
    u = lax.broadcasted_iota(jnp.int32, (TOK, TOK), 1)
    same = jnp.logical_and(ids_col == ids_row, u < t)
    before = jnp.max(jnp.where(same, 1, 0), axis=1, keepdims=True)
    return ids_col * MOST + before


def send_mask(idr_ref, idc_ref):
    slot = slot_of_row(idr_ref[0], idc_ref[0])
    rows = lax.broadcasted_iota(jnp.int32, (PER_HEAD, TOK), 0)
    return jnp.where(rows == slot, 1.0, 0.0).astype(BF16)


def take_mask(idr_ref, idc_ref):
    slot = slot_of_col(idr_ref[0], idc_ref[0])
    cols = lax.broadcasted_iota(jnp.int32, (TOK, PER_HEAD), 1)
    return jnp.where(cols == slot, 1.0, 0.0).astype(BF16)


def dispatch_qkv_kernel(idr_ref, idc_ref, q_ref, k_ref, v_ref, out_ref):
    mask = send_mask(idr_ref, idc_ref)
    whole = jnp.concatenate([q_ref[...], k_ref[...], v_ref[...], jnp.ones((TOK, DH), BF16)], axis=1)
    got = jnp.dot(mask, whole, preferred_element_type=F32)
    key = got[:, DH : 2 * DH] + EMPTY * (1.0 - got[:, 3 * DH :])
    out_ref[:, 0] = got[:, :DH].astype(BF16).reshape(OWNERS, ROWS, DH)
    out_ref[:, 1] = key.astype(BF16).reshape(OWNERS, ROWS, DH)
    out_ref[:, 2] = got[:, 2 * DH : 3 * DH].astype(BF16).reshape(OWNERS, ROWS, DH)


def dispatch_one_kernel(idr_ref, idc_ref, g_ref, out_ref):
    mask = send_mask(idr_ref, idc_ref)
    got = jnp.dot(mask, g_ref[...], preferred_element_type=F32)
    out_ref[...] = got.astype(BF16).reshape(OWNERS, ROWS, DH)


def combine_one_kernel(idr_ref, idc_ref, a_ref, out_ref):
    mask = take_mask(idr_ref, idc_ref)
    got = jnp.dot(mask, a_ref[...].reshape(PER_HEAD, DH), preferred_element_type=F32)
    out_ref[...] = got.astype(BF16)


def combine_grads_kernel(idr_ref, idc_ref, a_ref, dq_ref, dk_ref, dv_ref):
    mask = take_mask(idr_ref, idc_ref)
    whole = jnp.concatenate([a_ref[:, j].reshape(PER_HEAD, DH) for j in range(3)], axis=1)
    got = jnp.dot(mask, whole, preferred_element_type=F32).astype(BF16)
    dq_ref[...] = got[:, :DH]
    dk_ref[...] = got[:, DH : 2 * DH]
    dv_ref[...] = got[:, 2 * DH :]


def id_specs():
    return [
        pl.BlockSpec((1, 1, TOK), lambda h: (h, 0, 0)),
        pl.BlockSpec((1, TOK, 1), lambda h: (h, 0, 0)),
    ]


def token_spec():
    return pl.BlockSpec((TOK, DH), lambda h: (0, h))


def dispatch_qkv(idr, idc, q, k, v):
    return pl.pallas_call(
        dispatch_qkv_kernel,
        grid=(HEADS,),
        in_specs=id_specs() + [token_spec()] * 3,
        out_specs=pl.BlockSpec((OWNERS, 3, ROWS, DH), lambda h: (h, 0, 0, 0)),
        out_shape=jax.ShapeDtypeStruct((SEQ, 3, ROWS, DH), BF16),
        name="dispatch_qkv",
    )(idr, idc, q, k, v)


def dispatch_one(idr, idc, g):
    return pl.pallas_call(
        dispatch_one_kernel,
        grid=(HEADS,),
        in_specs=id_specs() + [token_spec()],
        out_specs=pl.BlockSpec((OWNERS, ROWS, DH), lambda h: (h, 0, 0)),
        out_shape=jax.ShapeDtypeStruct((SEQ, ROWS, DH), BF16),
        name="dispatch_one",
    )(idr, idc, g)


def combine_one(idr, idc, a):
    return pl.pallas_call(
        combine_one_kernel,
        grid=(HEADS,),
        in_specs=id_specs() + [pl.BlockSpec((OWNERS, ROWS, DH), lambda h: (h, 0, 0))],
        out_specs=token_spec(),
        out_shape=jax.ShapeDtypeStruct((TOK, HEADS * DH), BF16),
        name="combine_one",
    )(idr, idc, a)


def combine_grads(idr, idc, a):
    return pl.pallas_call(
        combine_grads_kernel,
        grid=(HEADS,),
        in_specs=id_specs() + [pl.BlockSpec((OWNERS, 3, ROWS, DH), lambda h: (h, 0, 0, 0))],
        out_specs=[token_spec()] * 3,
        out_shape=[jax.ShapeDtypeStruct((TOK, HEADS * DH), BF16)] * 3,
        name="combine_grads",
    )(idr, idc, a)


PB = GROUP * ROWS


def regroup_matrix(inverse):
    a = lax.broadcasted_iota(jnp.int32, (PB, PB), 1 if inverse else 0)
    b = lax.broadcasted_iota(jnp.int32, (PB, PB), 0 if inverse else 1)
    per = GROUP * MOST
    want = ((a % per) // MOST) * ROWS + (a // per) * MOST + a % MOST
    return jnp.where(b == want, 1.0, 0.0).astype(BF16)


def matmul(a, b, dims):
    return lax.dot_general(a, b, (dims, ((), ())), preferred_element_type=F32)


NT = ((1,), (1,))
NN = ((1,), (0,))
TN = ((0,), (0,))


def probabilities(q, k):
    scores = matmul(q, k, NT) * SCALE
    pick = jnp.where(lax.broadcasted_iota(jnp.int32, (8, DH), 1) == 0, 1.0, 0.0).astype(BF16)
    first = matmul(pick, k, NT)[0:1, :]
    t = lax.broadcasted_iota(jnp.int32, (SLOTS, SLOTS), 0)
    u = lax.broadcasted_iota(jnp.int32, (SLOTS, SLOTS), 1)
    allowed = jnp.logical_and(u <= t, first < 0.5 * EMPTY)
    scores = jnp.where(allowed, scores, NEGATIVE)
    weights = jnp.exp(scores - jnp.max(scores, axis=1, keepdims=True))
    return weights / jnp.sum(weights, axis=1, keepdims=True)


def regroup_in(perm, pieces, targets):
    whole = jnp.concatenate(pieces, axis=1)
    got = jnp.dot(perm, whole, preferred_element_type=F32).astype(BF16)
    return [got[:, i * DH : (i + 1) * DH].reshape(OWNED, GROUP * MOST, DH) for i in range(len(pieces))]


def forward_kernel(in_ref, qs_ref, ks_ref, vs_ref, out_ref, attn_ref):
    perm = regroup_matrix(False)
    for g in range(SEQ // GROUP):
        src = slice(g * GROUP, (g + 1) * GROUP)
        dst = slice(g * GROUP * MOST, (g + 1) * GROUP * MOST)
        pieces = [in_ref[src, j].reshape(PB, DH) for j in range(3)]
        q, k, v = regroup_in(perm, pieces, None)
        qs_ref[:, dst, :] = q
        ks_ref[:, dst, :] = k
        vs_ref[:, dst, :] = v

    def one(c, carry):
        p = probabilities(qs_ref[c], ks_ref[c]).astype(BF16)
        attn_ref[c] = matmul(p, vs_ref[c], NN).astype(BF16)
        return carry

    lax.fori_loop(0, OWNED, one, 0)
    back = regroup_matrix(True)
    for g in range(SEQ // GROUP):
        src = slice(g * GROUP, (g + 1) * GROUP)
        dst = slice(g * GROUP * MOST, (g + 1) * GROUP * MOST)
        y = attn_ref[:, dst, :].reshape(PB, DH)
        out_ref[src] = jnp.dot(back, y, preferred_element_type=F32).astype(BF16).reshape(GROUP, ROWS, DH)


def backward_kernel(g_ref, qs_ref, ks_ref, vs_ref, out_ref, gs_ref, dq_ref, dk_ref, dv_ref):
    perm = regroup_matrix(False)
    for g in range(SEQ // GROUP):
        src = slice(g * GROUP, (g + 1) * GROUP)
        dst = slice(g * GROUP * MOST, (g + 1) * GROUP * MOST)
        (gg,) = regroup_in(perm, [g_ref[src].reshape(PB, DH)], None)
        gs_ref[:, dst, :] = gg

    def one(c, carry):
        q, k, v, g = qs_ref[c], ks_ref[c], vs_ref[c], gs_ref[c]
        p = probabilities(q, k)
        dp = matmul(g, v, NT)
        delta = jnp.sum(p * dp, axis=1, keepdims=True)
        ds = (p * (dp - delta)).astype(BF16)
        dq_ref[c] = (matmul(ds, k, NN) * SCALE).astype(BF16)
        dk_ref[c] = (matmul(ds, q, TN) * SCALE).astype(BF16)
        dv_ref[c] = matmul(p.astype(BF16), g, TN).astype(BF16)
        return carry

    lax.fori_loop(0, OWNED, one, 0)
    back = regroup_matrix(True)
    for g in range(SEQ // GROUP):
        src = slice(g * GROUP, (g + 1) * GROUP)
        dst = slice(g * GROUP * MOST, (g + 1) * GROUP * MOST)
        y = jnp.concatenate([r[:, dst, :].reshape(PB, DH) for r in (dq_ref, dk_ref, dv_ref)], axis=1)
        got = jnp.dot(back, y, preferred_element_type=F32).astype(BF16)
        for j in range(3):
            out_ref[src, j] = got[:, j * DH : (j + 1) * DH].reshape(GROUP, ROWS, DH)


VM = pl.BlockSpec(memory_space=pltpu.VMEM)
GROUPED = (OWNED, SLOTS, DH)


def forward(received):
    return pl.pallas_call(
        forward_kernel,
        in_specs=[VM],
        out_specs=[VM] * 4,
        out_shape=[jax.ShapeDtypeStruct(GROUPED, BF16)] * 3 + [jax.ShapeDtypeStruct((SEQ, ROWS, DH), BF16)],
        scratch_shapes=[pltpu.VMEM(GROUPED, BF16)],
        name="cluster_forward",
    )(received)


def backward(received, qs, ks, vs):
    return pl.pallas_call(
        backward_kernel,
        in_specs=[VM] * 4,
        out_specs=VM,
        out_shape=jax.ShapeDtypeStruct((SEQ, 3, ROWS, DH), BF16),
        scratch_shapes=[pltpu.VMEM(GROUPED, BF16)] * 4,
        name="cluster_backward",
    )(received, qs, ks, vs)


def exchange(x):
    return lax.all_to_all(x, "seq", split_axis=0, concat_axis=0, tiled=True)


def body(query_rows, key_rows, value_rows, out_grad, cluster_ids, out_weight):
    idr = jnp.transpose(cluster_ids, (0, 2, 1))
    idc = cluster_ids
    qkv = exchange(dispatch_qkv(idr, idc, query_rows, key_rows, value_rows))
    attn_grad = lax.dot_general(
        out_grad, out_weight, (((1,), (1,)), ((), ())), preferred_element_type=F32
    ).astype(BF16)
    g_slots = exchange(dispatch_one(idr, idc, attn_grad))
    qs, ks, vs, attn_slots = forward(qkv)
    attn_back = exchange(attn_slots)
    grads_back = exchange(backward(g_slots, qs, ks, vs))
    attn = combine_one(idr, idc, attn_back)
    partial_out = jnp.dot(attn, out_weight, preferred_element_type=F32)
    half = partial_out.shape[1] // 2
    core = lax.axis_index("head")
    low, high = partial_out[:, :half], partial_out[:, half:]
    mine = jnp.where(core == 0, low, high)
    other = jnp.where(core == 0, high, low).astype(BF16)
    came = lax.ppermute(other, "head", [(0, 1), (1, 0)])
    layer_out = (mine + came.astype(F32)).astype(BF16)
    dq, dk, dv = combine_grads(idr, idc, grads_back)
    return layer_out, dq, dk, dv


def solution(mesh):
    in_specs = (
        P("seq", "head"),
        P("seq", "head"),
        P("seq", "head"),
        P("seq", None),
        P("head", "seq", None),
        P("head", None),
    )
    out_specs = (P("seq", "head"), P("seq", "head"), P("seq", "head"), P("seq", "head"))
    return jax.shard_map(body, mesh=mesh, in_specs=in_specs, out_specs=out_specs, check_vma=False)
```

```python
import jax
import jax.numpy as jnp
from jax import lax
from jax.experimental import pallas as pl
from jax.experimental.pallas import tpu as pltpu
from jax.sharding import PartitionSpec as P

CLUSTERS = 256
MOST = 2
DH = 128
SEQ = 128
HEADS = 8
TOK = 384
D = 2048
PER_HEAD = CLUSTERS * MOST
OWNERS = SEQ // HEADS
OWNED = CLUSTERS // OWNERS
ROWS = OWNED * MOST
SLOTS = SEQ * MOST
GROUP = 8
PAIR = 2
EMPTY = 64.0
NEGATIVE = -1e30
SCALE = DH ** -0.5
F32 = jnp.float32
BF16 = jnp.bfloat16

NT = ((1,), (1,))
NN = ((1,), (0,))
TN = ((0,), (0,))


def matmul(a, b, dims=NN):
    return lax.dot_general(a, b, (dims, ((), ())), preferred_element_type=F32)


def iota(shape, dim):
    return lax.broadcasted_iota(jnp.int32, shape, dim)


def dispatch_kernel(ids_ref, q_ref, k_ref, v_ref, og_ref, w_ref, out_ref):
    grad = matmul(og_ref[...], w_ref[...], NT).astype(BF16)
    before = jnp.where(iota((TOK, TOK), 0) < iota((TOK, TOK), 1), 1.0, 0.0).astype(BF16)
    for i in range(PAIR):
        lanes = slice(i * DH, (i + 1) * DH)
        owners = slice(i * OWNERS, (i + 1) * OWNERS)
        hit = jnp.where(iota((CLUSTERS, TOK), 0) == ids_ref[i], 1.0, 0.0)
        earlier = matmul(hit.astype(BF16), before)
        whole = jnp.concatenate([q_ref[:, lanes], k_ref[:, lanes], v_ref[:, lanes], grad[:, lanes]], axis=1)
        for m in range(MOST):
            mask = jnp.where(earlier == m, hit, 0.0)
            got = matmul(mask.astype(BF16), whole)
            used = jnp.sum(mask, axis=1, keepdims=True)
            rows = slice(m * OWNED, (m + 1) * OWNED)
            for j in range(4):
                part = got[:, j * DH : (j + 1) * DH]
                if j == 1:
                    part = part + EMPTY * (1.0 - used)
                out_ref[owners, j, rows, :] = part.astype(BF16).reshape(OWNERS, OWNED, DH)


def dispatch(ids, q, k, v, out_grad, weight):
    tokens = pl.BlockSpec((TOK, PAIR * DH), lambda h: (0, h))
    return pl.pallas_call(
        dispatch_kernel,
        grid=(HEADS // PAIR,),
        in_specs=[
            pl.BlockSpec((PAIR, 1, TOK), lambda h: (h, 0, 0)),
            tokens,
            tokens,
            tokens,
            pl.BlockSpec((TOK, D), lambda h: (0, 0)),
            pl.BlockSpec((PAIR * DH, D), lambda h: (h, 0)),
        ],
        out_specs=pl.BlockSpec((PAIR * OWNERS, 4, ROWS, DH), lambda h: (h, 0, 0, 0)),
        out_shape=jax.ShapeDtypeStruct((SEQ, 4, ROWS, DH), BF16),
        name="dispatch",
    )(ids, q, k, v, out_grad, weight)


def masks_kernel(idr_ref, idc_ref, out_ref):
    row, col = idr_ref[0], idc_ref[0]
    t, u = iota((TOK, TOK), 0), iota((TOK, TOK), 1)
    same = jnp.logical_and(col == row, u < t)
    earlier = jnp.max(jnp.where(same, 1, 0), axis=1, keepdims=True)
    slot = (col // OWNED) * ROWS + earlier * OWNED + col % OWNED
    out_ref[0] = jnp.where(iota((TOK, PER_HEAD), 1) == slot, 1.0, 0.0).astype(BF16)


def token_masks(idr, idc):
    return pl.pallas_call(
        masks_kernel,
        grid=(HEADS,),
        in_specs=[
            pl.BlockSpec((1, 1, TOK), lambda h: (h, 0, 0)),
            pl.BlockSpec((1, TOK, 1), lambda h: (h, 0, 0)),
        ],
        out_specs=pl.BlockSpec((1, TOK, PER_HEAD), lambda h: (h, 0, 0)),
        out_shape=jax.ShapeDtypeStruct((HEADS, TOK, PER_HEAD), BF16),
        name="token_masks",
    )(idr, idc)


PB = GROUP * ROWS
PER = GROUP * MOST


def regroup_matrix(inverse):
    a = iota((PB, PB), 1 if inverse else 0)
    b = iota((PB, PB), 0 if inverse else 1)
    want = ((a % PER) // MOST) * ROWS + (a % MOST) * OWNED + a // PER
    return jnp.where(b == want, 1.0, 0.0).astype(BF16)


def owner_kernel(in_ref, out_ref, q_ref, k_ref, v_ref, g_ref, o_ref, dq_ref, dk_ref, dv_ref):
    parts = (q_ref, k_ref, v_ref, g_ref)
    results = (o_ref, dq_ref, dk_ref, dv_ref)
    perm = regroup_matrix(False)
    for s in range(SEQ // GROUP):
        src = slice(s * GROUP, (s + 1) * GROUP)
        dst = slice(s * PER, (s + 1) * PER)
        whole = jnp.concatenate([in_ref[src, j].reshape(PB, DH) for j in range(4)], axis=1)
        got = matmul(perm, whole).astype(BF16)
        for j in range(4):
            parts[j][:, dst, :] = got[:, j * DH : (j + 1) * DH].reshape(OWNED, PER, DH)

    causal = iota((SLOTS, SLOTS), 0) <= iota((SLOTS, SLOTS), 1)

    def one(c):
        q, k, v, g = q_ref[c], k_ref[c], v_ref[c], g_ref[c]
        scores = matmul(k, q, NT) * SCALE
        allowed = jnp.logical_and(causal, k[:, 0:1].astype(F32) < 0.5 * EMPTY)
        scores = jnp.where(allowed, scores, NEGATIVE)
        weights = jnp.exp(scores - jnp.max(scores, axis=0, keepdims=True))
        probs = weights * (1.0 / jnp.sum(weights, axis=0, keepdims=True))
        half = probs.astype(BF16)
        dprob = matmul(v, g, NT)
        delta = jnp.sum(probs * dprob, axis=0, keepdims=True)
        ds = (probs * (dprob - delta)).astype(BF16)
        o_ref[c] = matmul(half, v, TN).astype(BF16)
        dv_ref[c] = matmul(half, g).astype(BF16)
        dk_ref[c] = (matmul(ds, q) * SCALE).astype(BF16)
        dq_ref[c] = (matmul(ds, k, TN) * SCALE).astype(BF16)

    def step(i, carry):
        one(2 * i)
        one(2 * i + 1)
        return carry

    lax.fori_loop(0, OWNED // 2, step, 0)
    back = regroup_matrix(True)
    for s in range(SEQ // GROUP):
        src = slice(s * GROUP, (s + 1) * GROUP)
        dst = slice(s * PER, (s + 1) * PER)
        whole = jnp.concatenate([r[:, dst, :].reshape(PB, DH) for r in results], axis=1)
        got = matmul(back, whole).astype(BF16)
        for j in range(4):
            out_ref[src, j] = got[:, j * DH : (j + 1) * DH].reshape(GROUP, ROWS, DH)


VM = pl.BlockSpec(memory_space=pltpu.VMEM)


def owner(received):
    return pl.pallas_call(
        owner_kernel,
        in_specs=[VM],
        out_specs=VM,
        out_shape=jax.ShapeDtypeStruct((SEQ, 4, ROWS, DH), BF16),
        scratch_shapes=[pltpu.VMEM((OWNED, SLOTS, DH), BF16)] * 8,
        name="owner",
    )(received)


def attn_kernel(core_ref, mask_ref, in_ref, w_ref, attn_ref, other_ref, acc_ref):
    h = pl.program_id(0)
    for i in range(PAIR):
        rows = in_ref[i * OWNERS : (i + 1) * OWNERS, 0].reshape(PER_HEAD, DH)
        attn_ref[:, i * DH : (i + 1) * DH] = matmul(mask_ref[i], rows).astype(BF16)
    part = matmul(attn_ref[...], w_ref[...])

    @pl.when(h == 0)
    def _():
        acc_ref[...] = part

    @pl.when(h > 0)
    def _():
        acc_ref[...] += part

    @pl.when(h == HEADS // PAIR - 1)
    def _():
        other_ref[...] = acc_ref[...].astype(BF16)


def attn_combine(core, masks, received, weight):
    return pl.pallas_call(
        attn_kernel,
        grid_spec=pltpu.PrefetchScalarGridSpec(
            num_scalar_prefetch=1,
            grid=(HEADS // PAIR,),
            in_specs=[
                pl.BlockSpec((PAIR, TOK, PER_HEAD), lambda h, core: (h, 0, 0)),
                pl.BlockSpec((PAIR * OWNERS, 1, ROWS, DH), lambda h, core: (h, 0, 0, 0)),
                pl.BlockSpec((PAIR * DH, D // 2), lambda h, core: (h, 1 - core[0])),
            ],
            out_specs=[
                pl.BlockSpec((TOK, PAIR * DH), lambda h, core: (0, h)),
                pl.BlockSpec((TOK, D // 2), lambda h, core: (0, 0)),
            ],
            scratch_shapes=[pltpu.VMEM((TOK, D // 2), F32)],
        ),
        out_shape=[
            jax.ShapeDtypeStruct((TOK, HEADS * DH), BF16),
            jax.ShapeDtypeStruct((TOK, D // 2), BF16),
        ],
        name="attn_combine",
    )(core, masks, received, weight)


def grads_kernel(mask_ref, in_ref, dq_ref, dk_ref, dv_ref):
    for i in range(PAIR):
        lanes = slice(i * DH, (i + 1) * DH)
        owners = slice(i * OWNERS, (i + 1) * OWNERS)
        whole = jnp.concatenate([in_ref[owners, j].reshape(PER_HEAD, DH) for j in (1, 2, 3)], axis=1)
        got = matmul(mask_ref[i], whole).astype(BF16)
        dq_ref[:, lanes] = got[:, :DH]
        dk_ref[:, lanes] = got[:, DH : 2 * DH]
        dv_ref[:, lanes] = got[:, 2 * DH :]


def grads_combine(masks, received):
    return pl.pallas_call(
        grads_kernel,
        grid=(HEADS // PAIR,),
        in_specs=[
            pl.BlockSpec((PAIR, TOK, PER_HEAD), lambda h: (h, 0, 0)),
            pl.BlockSpec((PAIR * OWNERS, 4, ROWS, DH), lambda h: (h, 0, 0, 0)),
        ],
        out_specs=[pl.BlockSpec((TOK, PAIR * DH), lambda h: (0, h))] * 3,
        out_shape=[jax.ShapeDtypeStruct((TOK, HEADS * DH), BF16)] * 3,
        name="grads_combine",
    )(masks, received)


def own_half_kernel(core_ref, attn_ref, w_ref, came_ref, out_ref):
    mine = matmul(attn_ref[...], w_ref[...])
    out_ref[...] = (mine + came_ref[...].astype(F32)).astype(BF16)


def own_half(core, attn, weight, came):
    width = 256
    steps = D // 2 // width
    return pl.pallas_call(
        own_half_kernel,
        grid_spec=pltpu.PrefetchScalarGridSpec(
            num_scalar_prefetch=1,
            grid=(steps,),
            in_specs=[
                pl.BlockSpec((TOK, HEADS * DH), lambda n, core: (0, 0)),
                pl.BlockSpec((HEADS * DH, width), lambda n, core: (0, core[0] * steps + n)),
                pl.BlockSpec((TOK, width), lambda n, core: (0, n)),
            ],
            out_specs=pl.BlockSpec((TOK, width), lambda n, core: (0, n)),
        ),
        out_shape=jax.ShapeDtypeStruct((TOK, D // 2), BF16),
        name="own_half",
    )(core, attn, weight, came)


def exchange(x):
    return lax.all_to_all(x, "seq", split_axis=0, concat_axis=0, tiled=True)


def body(query_rows, key_rows, value_rows, out_grad, cluster_ids, out_weight):
    idr = jnp.transpose(cluster_ids, (0, 2, 1))
    core = lax.axis_index("head").astype(jnp.int32).reshape(1)
    masks = token_masks(idr, cluster_ids)
    received = exchange(dispatch(idr, query_rows, key_rows, value_rows, out_grad, out_weight))
    back = exchange(owner(received))
    attn, other = attn_combine(core, masks, back, out_weight)
    came = lax.ppermute(other, "head", [(0, 1), (1, 0)])
    dq, dk, dv = grads_combine(masks, back)
    layer_out = own_half(core, attn, out_weight, came)
    return layer_out, dq, dk, dv


def solution(mesh):
    in_specs = (
        P("seq", "head"),
        P("seq", "head"),
        P("seq", "head"),
        P("seq", None),
        P("head", "seq", None),
        P("head", None),
    )
    out_specs = (P("seq", "head"), P("seq", "head"), P("seq", "head"), P("seq", "head"))
    return jax.shard_map(body, mesh=mesh, in_specs=in_specs, out_specs=out_specs, check_vma=False)
```

```python
import jax
import jax.numpy as jnp
from jax import lax
from jax.experimental import pallas as pl
from jax.experimental.pallas import tpu as pltpu
from jax.sharding import PartitionSpec as P

CLUSTERS = 256
MOST = 2
DH = 128
SEQ = 128
HEADS = 8
TOK = 384
D = 2048
PER_HEAD = CLUSTERS * MOST
OWNERS = SEQ // HEADS
OWNED = CLUSTERS // OWNERS
ROWS = OWNED * MOST
SLOTS = SEQ * MOST
GROUP = 8
PAIR = 2
EMPTY = 64.0
NEGATIVE = -1e30
SCALE = DH ** -0.5
F32 = jnp.float32
BF16 = jnp.bfloat16

NT = ((1,), (1,))
NN = ((1,), (0,))
TN = ((0,), (0,))


def matmul(a, b, dims=NN):
    return lax.dot_general(a, b, (dims, ((), ())), preferred_element_type=F32)


def iota(shape, dim):
    return lax.broadcasted_iota(jnp.int32, shape, dim)


def send_masks(ids):
    before = jnp.where(iota((TOK, TOK), 0) < iota((TOK, TOK), 1), 1.0, 0.0).astype(BF16)
    hit = jnp.where(iota((CLUSTERS, TOK), 0) == ids, 1.0, 0.0)
    earlier = matmul(hit.astype(BF16), before)
    return [jnp.where(earlier == m, hit, 0.0) for m in range(MOST)]


def dispatch_kernel(ids_ref, q_ref, k_ref, v_ref, out_ref):
    for i in range(PAIR):
        lanes = slice(i * DH, (i + 1) * DH)
        owners = slice(i * OWNERS, (i + 1) * OWNERS)
        whole = jnp.concatenate([q_ref[:, lanes], k_ref[:, lanes], v_ref[:, lanes]], axis=1)
        for m, mask in enumerate(send_masks(ids_ref[i])):
            got = matmul(mask.astype(BF16), whole)
            used = jnp.sum(mask, axis=1, keepdims=True)
            rows = slice(m * OWNED, (m + 1) * OWNED)
            for j in range(3):
                part = got[:, j * DH : (j + 1) * DH]
                if j == 1:
                    part = part + EMPTY * (1.0 - used)
                out_ref[owners, j, rows, :] = part.astype(BF16).reshape(OWNERS, OWNED, DH)


def grad_dispatch_kernel(ids_ref, og_ref, w_ref, out_ref):
    grad = matmul(og_ref[...], w_ref[...], NT).astype(BF16)
    for i in range(PAIR):
        owners = slice(i * OWNERS, (i + 1) * OWNERS)
        for m, mask in enumerate(send_masks(ids_ref[i])):
            got = matmul(mask.astype(BF16), grad[:, i * DH : (i + 1) * DH])
            rows = slice(m * OWNED, (m + 1) * OWNED)
            out_ref[owners, 0, rows, :] = got.astype(BF16).reshape(OWNERS, OWNED, DH)


def dispatch(ids, q, k, v):
    tokens = pl.BlockSpec((TOK, PAIR * DH), lambda h: (0, h))
    return pl.pallas_call(
        dispatch_kernel,
        grid=(HEADS // PAIR,),
        in_specs=[pl.BlockSpec((PAIR, 1, TOK), lambda h: (h, 0, 0)), tokens, tokens, tokens],
        out_specs=pl.BlockSpec((PAIR * OWNERS, 3, ROWS, DH), lambda h: (h, 0, 0, 0)),
        out_shape=jax.ShapeDtypeStruct((SEQ, 3, ROWS, DH), BF16),
        name="dispatch",
    )(ids, q, k, v)


def grad_dispatch(ids, out_grad, weight):
    return pl.pallas_call(
        grad_dispatch_kernel,
        grid=(HEADS // PAIR,),
        in_specs=[
            pl.BlockSpec((PAIR, 1, TOK), lambda h: (h, 0, 0)),
            pl.BlockSpec((TOK, D), lambda h: (0, 0)),
            pl.BlockSpec((PAIR * DH, D), lambda h: (h, 0)),
        ],
        out_specs=pl.BlockSpec((PAIR * OWNERS, 1, ROWS, DH), lambda h: (h, 0, 0, 0)),
        out_shape=jax.ShapeDtypeStruct((SEQ, 1, ROWS, DH), BF16),
        name="grad_dispatch",
    )(ids, out_grad, weight)


def masks_kernel(idr_ref, idc_ref, out_ref):
    row, col = idr_ref[0], idc_ref[0]
    t, u = iota((TOK, TOK), 0), iota((TOK, TOK), 1)
    same = jnp.logical_and(col == row, u < t)
    earlier = jnp.max(jnp.where(same, 1, 0), axis=1, keepdims=True)
    slot = (col // OWNED) * ROWS + earlier * OWNED + col % OWNED
    out_ref[0] = jnp.where(iota((TOK, PER_HEAD), 1) == slot, 1.0, 0.0).astype(BF16)


def token_masks(idr, idc):
    return pl.pallas_call(
        masks_kernel,
        grid=(HEADS,),
        in_specs=[
            pl.BlockSpec((1, 1, TOK), lambda h: (h, 0, 0)),
            pl.BlockSpec((1, TOK, 1), lambda h: (h, 0, 0)),
        ],
        out_specs=pl.BlockSpec((1, TOK, PER_HEAD), lambda h: (h, 0, 0)),
        out_shape=jax.ShapeDtypeStruct((HEADS, TOK, PER_HEAD), BF16),
        name="token_masks",
    )(idr, idc)


PB = GROUP * ROWS
PER = GROUP * MOST


def regroup_matrix(inverse):
    a = iota((PB, PB), 1 if inverse else 0)
    b = iota((PB, PB), 0 if inverse else 1)
    want = ((a % PER) // MOST) * ROWS + (a % MOST) * OWNED + a // PER
    return jnp.where(b == want, 1.0, 0.0).astype(BF16)


def each(count, unroll, fn):
    def step(i, carry):
        for n in range(unroll):
            fn(i * unroll + n)
        return carry

    lax.fori_loop(0, count // unroll, step, 0)


def regroup_in(in_ref, targets):
    perm = regroup_matrix(False)
    width = len(targets)
    for s in range(SEQ // GROUP):
        src = slice(s * GROUP, (s + 1) * GROUP)
        dst = slice(s * PER, (s + 1) * PER)
        whole = jnp.concatenate([in_ref[src, j].reshape(PB, DH) for j in range(width)], axis=1)
        got = matmul(perm, whole).astype(BF16)
        for j in range(width):
            targets[j][:, dst, :] = got[:, j * DH : (j + 1) * DH].reshape(OWNED, PER, DH)


def regroup_out(results, out_ref):
    back = regroup_matrix(True)
    for s in range(SEQ // GROUP):
        src = slice(s * GROUP, (s + 1) * GROUP)
        dst = slice(s * PER, (s + 1) * PER)
        whole = jnp.concatenate([r[:, dst, :].reshape(PB, DH) for r in results], axis=1)
        got = matmul(back, whole).astype(BF16)
        for j in range(len(results)):
            out_ref[src, j] = got[:, j * DH : (j + 1) * DH].reshape(GROUP, ROWS, DH)


def probabilities(q, k):
    causal = iota((SLOTS, SLOTS), 0) <= iota((SLOTS, SLOTS), 1)
    scores = matmul(k, q, NT) * SCALE
    allowed = jnp.logical_and(causal, k[:, 0:1].astype(F32) < 0.5 * EMPTY)
    scores = jnp.where(allowed, scores, NEGATIVE)
    weights = jnp.exp(scores - jnp.max(scores, axis=0, keepdims=True))
    return weights * (1.0 / jnp.sum(weights, axis=0, keepdims=True))


def forward_kernel(in_ref, q_ref, k_ref, v_ref, out_ref, o_ref):
    regroup_in(in_ref, (q_ref, k_ref, v_ref))

    def one(c):
        half = probabilities(q_ref[c], k_ref[c]).astype(BF16)
        o_ref[c] = matmul(half, v_ref[c], TN).astype(BF16)

    each(OWNED, 2, one)
    regroup_out((o_ref,), out_ref)


def backward_kernel(in_ref, q_ref, k_ref, v_ref, out_ref, g_ref, dq_ref, dk_ref, dv_ref):
    regroup_in(in_ref, (g_ref,))

    def one(c):
        q, k, v, g = q_ref[c], k_ref[c], v_ref[c], g_ref[c]
        probs = probabilities(q, k)
        dprob = matmul(v, g, NT)
        delta = jnp.sum(probs * dprob, axis=0, keepdims=True)
        ds = (probs * (dprob - delta)).astype(BF16)
        dv_ref[c] = matmul(probs.astype(BF16), g).astype(BF16)
        dk_ref[c] = (matmul(ds, q) * SCALE).astype(BF16)
        dq_ref[c] = (matmul(ds, k, TN) * SCALE).astype(BF16)

    each(OWNED, 2, one)
    regroup_out((dq_ref, dk_ref, dv_ref), out_ref)


VM = pl.BlockSpec(memory_space=pltpu.VMEM)
GROUPED = (OWNED, SLOTS, DH)


def forward(received):
    return pl.pallas_call(
        forward_kernel,
        in_specs=[VM],
        out_specs=[VM] * 4,
        out_shape=[jax.ShapeDtypeStruct(GROUPED, BF16)] * 3 + [jax.ShapeDtypeStruct((SEQ, 1, ROWS, DH), BF16)],
        scratch_shapes=[pltpu.VMEM(GROUPED, BF16)],
        name="cluster_forward",
    )(received)


def backward(received, q, k, v):
    return pl.pallas_call(
        backward_kernel,
        in_specs=[VM] * 4,
        out_specs=VM,
        out_shape=jax.ShapeDtypeStruct((SEQ, 3, ROWS, DH), BF16),
        scratch_shapes=[pltpu.VMEM(GROUPED, BF16)] * 4,
        name="cluster_backward",
    )(received, q, k, v)


def attn_kernel(core_ref, mask_ref, in_ref, w_ref, attn_ref, other_ref, acc_ref):
    h = pl.program_id(0)
    for i in range(PAIR):
        owners = pl.ds((h * PAIR + i) * OWNERS, OWNERS)
        rows = in_ref[owners, 0].reshape(PER_HEAD, DH)
        attn_ref[:, i * DH : (i + 1) * DH] = matmul(mask_ref[i], rows).astype(BF16)
    part = matmul(attn_ref[...], w_ref[...])

    @pl.when(h == 0)
    def _():
        acc_ref[...] = part

    @pl.when(h > 0)
    def _():
        acc_ref[...] += part

    @pl.when(h == HEADS // PAIR - 1)
    def _():
        other_ref[...] = acc_ref[...].astype(BF16)


def attn_combine(core, masks, received, weight):
    return pl.pallas_call(
        attn_kernel,
        grid_spec=pltpu.PrefetchScalarGridSpec(
            num_scalar_prefetch=1,
            grid=(HEADS // PAIR,),
            in_specs=[
                pl.BlockSpec((PAIR, TOK, PER_HEAD), lambda h, core: (h, 0, 0)),
                VM,
                pl.BlockSpec((PAIR * DH, D // 2), lambda h, core: (h, 1 - core[0])),
            ],
            out_specs=[
                pl.BlockSpec((TOK, PAIR * DH), lambda h, core: (0, h)),
                pl.BlockSpec((TOK, D // 2), lambda h, core: (0, 0)),
            ],
            scratch_shapes=[pltpu.VMEM((TOK, D // 2), F32)],
        ),
        out_shape=[
            jax.ShapeDtypeStruct((TOK, HEADS * DH), BF16),
            jax.ShapeDtypeStruct((TOK, D // 2), BF16),
        ],
        name="attn_combine",
    )(core, masks, received, weight)


def grads_kernel(mask_ref, in_ref, dq_ref, dk_ref, dv_ref):
    for i in range(PAIR):
        lanes = slice(i * DH, (i + 1) * DH)
        owners = pl.ds((pl.program_id(0) * PAIR + i) * OWNERS, OWNERS)
        whole = jnp.concatenate([in_ref[owners, j].reshape(PER_HEAD, DH) for j in range(3)], axis=1)
        got = matmul(mask_ref[i], whole).astype(BF16)
        dq_ref[:, lanes] = got[:, :DH]
        dk_ref[:, lanes] = got[:, DH : 2 * DH]
        dv_ref[:, lanes] = got[:, 2 * DH :]


def grads_combine(masks, received):
    return pl.pallas_call(
        grads_kernel,
        grid=(HEADS // PAIR,),
        in_specs=[
            pl.BlockSpec((PAIR, TOK, PER_HEAD), lambda h: (h, 0, 0)),
            VM,
        ],
        out_specs=[pl.BlockSpec((TOK, PAIR * DH), lambda h: (0, h))] * 3,
        out_shape=[jax.ShapeDtypeStruct((TOK, HEADS * DH), BF16)] * 3,
        name="grads_combine",
    )(masks, received)


def own_half_kernel(core_ref, attn_ref, w_ref, came_ref, out_ref):
    mine = matmul(attn_ref[...], w_ref[...])
    out_ref[...] = (mine + came_ref[...].astype(F32)).astype(BF16)


def own_half(core, attn, weight, came):
    width = 256
    steps = D // 2 // width
    return pl.pallas_call(
        own_half_kernel,
        grid_spec=pltpu.PrefetchScalarGridSpec(
            num_scalar_prefetch=1,
            grid=(steps,),
            in_specs=[
                pl.BlockSpec((TOK, HEADS * DH), lambda n, core: (0, 0)),
                pl.BlockSpec((HEADS * DH, width), lambda n, core: (0, core[0] * steps + n)),
                pl.BlockSpec((TOK, width), lambda n, core: (0, n)),
            ],
            out_specs=pl.BlockSpec((TOK, width), lambda n, core: (0, n)),
        ),
        out_shape=jax.ShapeDtypeStruct((TOK, D // 2), BF16),
        name="own_half",
    )(core, attn, weight, came)


def exchange(x):
    got = lax.all_to_all(x, "seq", split_axis=0, concat_axis=0, tiled=True)
    return pltpu.with_memory_space_constraint(got, pltpu.MemorySpace.VMEM)


def body(query_rows, key_rows, value_rows, out_grad, cluster_ids, out_weight):
    idr = jnp.transpose(cluster_ids, (0, 2, 1))
    core = lax.axis_index("head").astype(jnp.int32).reshape(1)
    masks = token_masks(idr, cluster_ids)
    received = exchange(dispatch(idr, query_rows, key_rows, value_rows))
    grads_in = exchange(grad_dispatch(idr, out_grad, out_weight))
    q, k, v, attn_out = forward(received)
    attn_back = exchange(attn_out)
    back = exchange(backward(grads_in, q, k, v))
    attn, other = attn_combine(core, masks, attn_back, out_weight)
    came = lax.ppermute(other, "head", [(0, 1), (1, 0)])
    layer_out = own_half(core, attn, out_weight, came)
    dq, dk, dv = grads_combine(masks, back)
    return layer_out, dq, dk, dv


def solution(mesh):
    in_specs = (
        P("seq", "head"),
        P("seq", "head"),
        P("seq", "head"),
        P("seq", None),
        P("head", "seq", None),
        P("head", None),
    )
    out_specs = (P("seq", "head"), P("seq", "head"), P("seq", "head"), P("seq", "head"))
    return jax.shard_map(body, mesh=mesh, in_specs=in_specs, out_specs=out_specs, check_vma=False)
```

```python
import jax
import jax.numpy as jnp
from jax import lax
from jax.experimental import pallas as pl
from jax.experimental.pallas import tpu as pltpu
from jax.sharding import PartitionSpec as P

CLUSTERS = 256
MOST = 2
DH = 128
SEQ = 128
HEADS = 8
TOK = 384
D = 2048
PER_HEAD = CLUSTERS * MOST
OWNERS = SEQ // HEADS
OWNED = CLUSTERS // OWNERS
ROWS = OWNED * MOST
SLOTS = SEQ * MOST
GROUP = 8
PAIR = 2
STEP = 4
PARTS = 4
EMPTY = 64.0
NEGATIVE = -1e30
SCALE = DH ** -0.5
F32 = jnp.float32
BF16 = jnp.bfloat16

VM = pl.BlockSpec(memory_space=pltpu.VMEM)
ANY = pl.BlockSpec(memory_space=pl.ANY)

NT = ((1,), (1,))
NN = ((1,), (0,))
TN = ((0,), (0,))


def matmul(a, b, dims=NN):
    return lax.dot_general(a, b, (dims, ((), ())), preferred_element_type=F32)


def iota(shape, dim):
    return lax.broadcasted_iota(jnp.int32, shape, dim)


def send_masks(ids):
    before = jnp.where(iota((TOK, TOK), 0) < iota((TOK, TOK), 1), 1.0, 0.0).astype(BF16)
    hit = jnp.where(iota((CLUSTERS, TOK), 0) == ids, 1.0, 0.0)
    earlier = matmul(hit.astype(BF16), before)
    return [jnp.where(earlier == m, hit, 0.0) for m in range(MOST)]


def dispatch_kernel(ids_ref, q_hbm, k_hbm, v_hbm, og_hbm, w_hbm, out_hbm, q_ref, k_ref, v_ref, og_ref, w_ref, buf_ref, mask_ref, in_sem, w_sem, out_sem):
    half = STEP * DH
    ins = [pltpu.make_async_copy(a, b, in_sem.at[i]) for i, (a, b) in enumerate(((og_hbm, og_ref), (q_hbm, q_ref), (k_hbm, k_ref), (v_hbm, v_ref)))]
    ws = [pltpu.make_async_copy(w_hbm.at[pl.ds(n * half, half)], w_ref.at[pl.ds(n * half, half)], w_sem.at[n]) for n in range(HEADS // STEP)]
    ins[0].start()
    ws[0].start()
    for c in ins[1:]:
        c.start()
    for c in ws[1:]:
        c.start()
    for h in range(HEADS):
        for m, mask in enumerate(send_masks(ids_ref[h])):
            mask_ref[h, m] = mask.astype(BF16)
    ins[0].wait()
    outs = []
    for n in range(HEADS // STEP):
        ws[n].wait()
        grad = matmul(og_ref[...], w_ref[n * half : (n + 1) * half], NT).astype(BF16)
        if n == 0:
            for c in ins[1:]:
                c.wait()
        for i in range(STEP):
            h = n * STEP + i
            lanes = slice(h * DH, (h + 1) * DH)
            owners = slice(h * OWNERS, (h + 1) * OWNERS)
            whole = jnp.concatenate([q_ref[:, lanes], k_ref[:, lanes], v_ref[:, lanes], grad[:, i * DH : (i + 1) * DH]], axis=1)
            for m in range(MOST):
                mask = mask_ref[h, m]
                got = matmul(mask, whole)
                used = jnp.sum(mask.astype(F32), axis=1, keepdims=True)
                rows = slice(m * OWNED, (m + 1) * OWNED)
                for j in range(4):
                    part = got[:, j * DH : (j + 1) * DH]
                    if j == 1:
                        part = part + EMPTY * (1.0 - used)
                    buf_ref[owners, j, rows, :] = part.astype(BF16).reshape(OWNERS, OWNED, DH)
            c = pltpu.make_async_copy(buf_ref.at[pl.ds(h * OWNERS, OWNERS)], out_hbm.at[pl.ds(h * OWNERS, OWNERS)], out_sem.at[h])
            c.start()
            outs.append(c)
    for c in outs:
        c.wait()


def dispatch(ids, q, k, v, og, w):
    tok = pltpu.VMEM((TOK, HEADS * DH), BF16)
    return pl.pallas_call(
        dispatch_kernel,
        in_specs=[VM] + [ANY] * 5,
        out_specs=ANY,
        out_shape=jax.ShapeDtypeStruct((SEQ, 4, ROWS, DH), BF16),
        scratch_shapes=[tok, tok, tok, pltpu.VMEM((TOK, D), BF16), pltpu.VMEM((HEADS * DH, D), BF16), pltpu.VMEM((SEQ, 4, ROWS, DH), BF16),
            pltpu.VMEM((HEADS, MOST, CLUSTERS, TOK), BF16), pltpu.SemaphoreType.DMA((4,)), pltpu.SemaphoreType.DMA((HEADS // STEP,)), pltpu.SemaphoreType.DMA((HEADS,))],
        name="dispatch",
    )(ids, q, k, v, og, w)


def masks_kernel(idr_ref, idc_ref, out_ref):
    row, col = idr_ref[0], idc_ref[0]
    t, u = iota((TOK, TOK), 0), iota((TOK, TOK), 1)
    same = jnp.logical_and(col == row, u < t)
    earlier = jnp.max(jnp.where(same, 1, 0), axis=1, keepdims=True)
    slot = (col // OWNED) * ROWS + earlier * OWNED + col % OWNED
    out_ref[0] = jnp.where(iota((TOK, PER_HEAD), 1) == slot, 1.0, 0.0).astype(BF16)


def token_masks(idr, idc):
    return pl.pallas_call(
        masks_kernel,
        grid=(HEADS,),
        in_specs=[
            pl.BlockSpec((1, 1, TOK), lambda h: (h, 0, 0)),
            pl.BlockSpec((1, TOK, 1), lambda h: (h, 0, 0)),
        ],
        out_specs=pl.BlockSpec((1, TOK, PER_HEAD), lambda h: (h, 0, 0)),
        out_shape=jax.ShapeDtypeStruct((HEADS, TOK, PER_HEAD), BF16),
        name="token_masks",
    )(idr, idc)


PB = GROUP * ROWS
PER = GROUP * MOST


def regroup_matrix(inverse):
    a = iota((PB, PB), 1 if inverse else 0)
    b = iota((PB, PB), 0 if inverse else 1)
    want = ((a % PER) // MOST) * ROWS + (a % MOST) * OWNED + a // PER
    return jnp.where(b == want, 1.0, 0.0).astype(BF16)


def each(count, unroll, fn):
    def step(i, carry):
        for n in range(unroll):
            fn(i * unroll + n)
        return carry

    lax.fori_loop(0, count // unroll, step, 0)


def regroup_in(in_ref, targets):
    perm = regroup_matrix(False)
    width = len(targets)
    for s in range(SEQ // GROUP):
        src = slice(s * GROUP, (s + 1) * GROUP)
        dst = slice(s * PER, (s + 1) * PER)
        whole = jnp.concatenate([in_ref[src, j].reshape(PB, DH) for j in range(width)], axis=1)
        got = matmul(perm, whole).astype(BF16)
        for j in range(width):
            targets[j][:, dst, :] = got[:, j * DH : (j + 1) * DH].reshape(OWNED, PER, DH)


def regroup_out(results, out_ref):
    back = regroup_matrix(True)
    for s in range(SEQ // GROUP):
        src = slice(s * GROUP, (s + 1) * GROUP)
        dst = slice(s * PER, (s + 1) * PER)
        whole = jnp.concatenate([r[:, dst, :].reshape(PB, DH) for r in results], axis=1)
        got = matmul(back, whole).astype(BF16)
        for j in range(len(results)):
            out_ref[src, j] = got[:, j * DH : (j + 1) * DH].reshape(GROUP, ROWS, DH)


def probabilities(q, k):
    causal = iota((SLOTS, SLOTS), 0) <= iota((SLOTS, SLOTS), 1)
    scores = matmul(k, q, NT) * SCALE
    allowed = jnp.logical_and(causal, k[:, 0:1].astype(F32) < 0.5 * EMPTY)
    scores = jnp.where(allowed, scores, NEGATIVE)
    weights = jnp.exp(scores - jnp.max(scores, axis=0, keepdims=True))
    return weights * (1.0 / jnp.sum(weights, axis=0, keepdims=True))


GROUPED = (OWNED, SLOTS, DH)


def load_parts(in_hbm, buf, sem, js):
    each_src = SEQ // PARTS
    cs = []
    for n in range(PARTS):
        src = pl.ds(n * each_src, each_src)
        c = pltpu.make_async_copy(in_hbm.at[src, js], buf.at[src], sem.at[n])
        c.start(); cs.append(c)
    return cs

def forward_kernel(in_hbm, out_ref, buf_ref, q_ref, k_ref, v_ref, o_ref, sem):
    cs = load_parts(in_hbm, buf_ref, sem, pl.ds(0, 3))
    perm = regroup_matrix(False)
    per = SEQ // GROUP // PARTS
    targets = (q_ref, k_ref, v_ref)
    for s in range(SEQ // GROUP):
        if s % per == 0:
            cs[s // per].wait()
        src = slice(s * GROUP, (s + 1) * GROUP)
        dst = slice(s * PER, (s + 1) * PER)
        whole = jnp.concatenate([buf_ref[src, j].reshape(PB, DH) for j in range(3)], axis=1)
        got = matmul(perm, whole).astype(BF16)
        for j in range(3):
            targets[j][:, dst, :] = got[:, j * DH : (j + 1) * DH].reshape(OWNED, PER, DH)
    def one(c):
        half = probabilities(q_ref[c], k_ref[c]).astype(BF16)
        o_ref[c] = matmul(half, v_ref[c], TN).astype(BF16)
    each(OWNED, 16, one)
    regroup_out((o_ref,), out_ref)


def forward(received):
    return pl.pallas_call(
        forward_kernel,
        in_specs=[ANY],
        out_specs=VM,
        out_shape=jax.ShapeDtypeStruct((SEQ, 1, ROWS, DH), BF16),
        scratch_shapes=[pltpu.VMEM((SEQ, 3, ROWS, DH), BF16)] + [pltpu.VMEM(GROUPED, BF16)] * 4 + [pltpu.SemaphoreType.DMA((PARTS,))],
        name="cluster_forward",
    )(received)


def backward_kernel(in_ref, out_ref, q_ref, k_ref, v_ref, g_ref, dq_ref, dk_ref, dv_ref):
    regroup_in(in_ref, (q_ref, k_ref, v_ref, g_ref))
    def one(c):
        q, k, v, g = q_ref[c], k_ref[c], v_ref[c], g_ref[c]
        probs = probabilities(q, k)
        dprob = matmul(v, g, NT)
        delta = jnp.sum(probs * dprob, axis=0, keepdims=True)
        ds = (probs * (dprob - delta)).astype(BF16)
        dv_ref[c] = matmul(probs.astype(BF16), g).astype(BF16)
        dk_ref[c] = (matmul(ds, q) * SCALE).astype(BF16)
        dq_ref[c] = (matmul(ds, k, TN) * SCALE).astype(BF16)
    each(OWNED, 8, one)
    regroup_out((dq_ref, dk_ref, dv_ref), out_ref)


def backward(received):
    return pl.pallas_call(
        backward_kernel,
        in_specs=[VM],
        out_specs=VM,
        out_shape=jax.ShapeDtypeStruct((SEQ, 3, ROWS, DH), BF16),
        scratch_shapes=[pltpu.VMEM(GROUPED, BF16)] * 7,
        name="cluster_backward",
    )(received)


def attn_kernel(core_ref, mask_ref, in_ref, w_ref, attn_ref, other_ref, acc_ref):
    h = pl.program_id(0)
    for i in range(PAIR):
        owners = pl.ds((h * PAIR + i) * OWNERS, OWNERS)
        rows = in_ref[owners, 0].reshape(PER_HEAD, DH)
        attn_ref[:, i * DH : (i + 1) * DH] = matmul(mask_ref[i], rows).astype(BF16)
    part = matmul(attn_ref[...], w_ref[...])

    @pl.when(h == 0)
    def _():
        acc_ref[...] = part

    @pl.when(h > 0)
    def _():
        acc_ref[...] += part

    @pl.when(h == HEADS // PAIR - 1)
    def _():
        other_ref[...] = acc_ref[...].astype(BF16)


def attn_combine(core, masks, received, weight):
    return pl.pallas_call(
        attn_kernel,
        grid_spec=pltpu.PrefetchScalarGridSpec(
            num_scalar_prefetch=1,
            grid=(HEADS // PAIR,),
            in_specs=[
                pl.BlockSpec((PAIR, TOK, PER_HEAD), lambda h, core: (h, 0, 0)),
                VM,
                pl.BlockSpec((PAIR * DH, D // 2), lambda h, core: (h, 1 - core[0])),
            ],
            out_specs=[
                pl.BlockSpec((TOK, PAIR * DH), lambda h, core: (0, h)),
                pl.BlockSpec((TOK, D // 2), lambda h, core: (0, 0)),
            ],
            scratch_shapes=[pltpu.VMEM((TOK, D // 2), F32)],
        ),
        out_shape=[
            jax.ShapeDtypeStruct((TOK, HEADS * DH), BF16),
            jax.ShapeDtypeStruct((TOK, D // 2), BF16),
        ],
        name="attn_combine",
    )(core, masks, received, weight)


def grads_kernel(mask_hbm, in_hbm, dq_hbm, dk_hbm, dv_hbm, mask_ref, buf_ref, out_ref, in_sem, out_sem):
    outs = (dq_hbm, dk_hbm, dv_hbm)
    ins = []
    for h in range(HEADS):
        owners = pl.ds(h * OWNERS, OWNERS)
        a = pltpu.make_async_copy(mask_hbm.at[h], mask_ref.at[h], in_sem.at[h, 0])
        b = pltpu.make_async_copy(in_hbm.at[owners], buf_ref.at[owners], in_sem.at[h, 1])
        a.start()
        b.start()
        ins.append((a, b))
    sent = []
    for h in range(HEADS):
        for c in ins[h]:
            c.wait()
        owners = slice(h * OWNERS, (h + 1) * OWNERS)
        whole = jnp.concatenate([buf_ref[owners, j].reshape(PER_HEAD, DH) for j in range(3)], axis=1)
        got = matmul(mask_ref[h], whole).astype(BF16)
        for j in range(3):
            out_ref[j, :, h * DH : (h + 1) * DH] = got[:, j * DH : (j + 1) * DH]
        if h % PAIR == PAIR - 1:
            n = h // PAIR
            lanes = pl.ds(n * PAIR * DH, PAIR * DH)
            for j in range(3):
                c = pltpu.make_async_copy(out_ref.at[j, :, lanes], outs[j].at[:, lanes], out_sem.at[n, j])
                c.start()
                sent.append(c)
    for c in sent:
        c.wait()


def grads_combine(masks, received):
    return pl.pallas_call(
        grads_kernel,
        in_specs=[ANY] * 2,
        out_specs=[ANY] * 3,
        out_shape=[jax.ShapeDtypeStruct((TOK, HEADS * DH), BF16)] * 3,
        scratch_shapes=[
            pltpu.VMEM((HEADS, TOK, PER_HEAD), BF16),
            pltpu.VMEM((SEQ, 3, ROWS, DH), BF16),
            pltpu.VMEM((3, TOK, HEADS * DH), BF16),
            pltpu.SemaphoreType.DMA((HEADS, 2)),
            pltpu.SemaphoreType.DMA((HEADS // PAIR, 3)),
        ],
        name="grads_combine",
    )(masks, received)


def own_half_kernel(core_ref, attn_ref, w_ref, came_ref, out_ref):
    mine = matmul(attn_ref[...], w_ref[...])
    out_ref[...] = (mine + came_ref[...].astype(F32)).astype(BF16)


def own_half(core, attn, weight, came):
    width = 256
    steps = D // 2 // width
    return pl.pallas_call(
        own_half_kernel,
        grid_spec=pltpu.PrefetchScalarGridSpec(
            num_scalar_prefetch=1,
            grid=(steps,),
            in_specs=[
                pl.BlockSpec((TOK, HEADS * DH), lambda n, core: (0, 0)),
                pl.BlockSpec((HEADS * DH, width), lambda n, core: (0, core[0] * steps + n)),
                pl.BlockSpec((TOK, width), lambda n, core: (0, n)),
            ],
            out_specs=pl.BlockSpec((TOK, width), lambda n, core: (0, n)),
        ),
        out_shape=jax.ShapeDtypeStruct((TOK, D // 2), BF16),
        name="own_half",
    )(core, attn, weight, came)


def exchange(x):
    return lax.all_to_all(x, "seq", split_axis=0, concat_axis=0, tiled=True)


def in_vmem(x):
    return pltpu.with_memory_space_constraint(x, pltpu.MemorySpace.VMEM)


def body(query_rows, key_rows, value_rows, out_grad, cluster_ids, out_weight):
    idr = jnp.transpose(cluster_ids, (0, 2, 1))
    core = lax.axis_index("head").astype(jnp.int32).reshape(1)
    masks = token_masks(idr, cluster_ids)
    received = exchange(dispatch(idr, query_rows, key_rows, value_rows, out_grad, out_weight))
    attn_back = in_vmem(exchange(forward(received)))
    back = exchange(backward(received))
    attn, other = attn_combine(core, masks, attn_back, out_weight)
    came = lax.ppermute(other, "head", [(0, 1), (1, 0)])
    layer_out = own_half(core, attn, out_weight, came)
    dq, dk, dv = grads_combine(masks, back)
    return layer_out, dq, dk, dv


def solution(mesh):
    in_specs = (
        P("seq", "head"),
        P("seq", "head"),
        P("seq", "head"),
        P("seq", None),
        P("head", "seq", None),
        P("head", None),
    )
    out_specs = (P("seq", "head"), P("seq", "head"), P("seq", "head"), P("seq", "head"))
    return jax.shard_map(body, mesh=mesh, in_specs=in_specs, out_specs=out_specs, check_vma=False)
```

```python
import jax
import jax.numpy as jnp
from jax import lax
from jax.experimental import pallas as pl
from jax.experimental.pallas import tpu as pltpu
from jax.sharding import PartitionSpec as P

CLUSTERS = 256
MOST = 2
DH = 128
SEQ = 128
HEADS = 8
TOK = 384
D = 2048
PER_HEAD = CLUSTERS * MOST
OWNERS = SEQ // HEADS
OWNED = CLUSTERS // OWNERS
ROWS = OWNED * MOST
SLOTS = SEQ * MOST
GROUP = 8
PAIR = 2
STEP = 4
PARTS = 4
STAGGER_NS = 20000
EMPTY = 64.0
NEGATIVE = -1e30
SCALE = DH ** -0.5
F32 = jnp.float32
BF16 = jnp.bfloat16

VM = pl.BlockSpec(memory_space=pltpu.VMEM)
ANY = pl.BlockSpec(memory_space=pl.ANY)

NT = ((1,), (1,))
NN = ((1,), (0,))
TN = ((0,), (0,))


def matmul(a, b, dims=NN):
    return lax.dot_general(a, b, (dims, ((), ())), preferred_element_type=F32)


def iota(shape, dim):
    return lax.broadcasted_iota(jnp.int32, shape, dim)


def send_masks(ids):
    before = jnp.where(iota((TOK, TOK), 0) < iota((TOK, TOK), 1), 1.0, 0.0).astype(BF16)
    hit = jnp.where(iota((CLUSTERS, TOK), 0) == ids, 1.0, 0.0)
    earlier = matmul(hit.astype(BF16), before)
    return [jnp.where(earlier == m, hit, 0.0) for m in range(MOST)]


def dispatch_kernel(core_ref, ids_ref, q_hbm, k_hbm, v_hbm, og_hbm, w_hbm, out_hbm, q_ref, k_ref, v_ref, og_ref, w_ref, buf_ref, mask_ref, in_sem, w_sem, out_sem):
    half = STEP * DH
    ins = [pltpu.make_async_copy(a, b, in_sem.at[i]) for i, (a, b) in enumerate(((og_hbm, og_ref), (q_hbm, q_ref), (k_hbm, k_ref), (v_hbm, v_ref)))]
    ws = [pltpu.make_async_copy(w_hbm.at[pl.ds(n * half, half)], w_ref.at[pl.ds(n * half, half)], w_sem.at[n]) for n in range(HEADS // STEP)]
    ins[0].start()
    ws[0].start()
    for c in ins[1:]:
        c.start()
    for c in ws[1:]:
        c.start()

    @pl.when(core_ref[0] == 1)
    def _():
        pl.delay(STAGGER_NS)

    for h in range(HEADS):
        for m, mask in enumerate(send_masks(ids_ref[h])):
            mask_ref[h, m] = mask.astype(BF16)
    ins[0].wait()
    outs = []
    for n in range(HEADS // STEP):
        ws[n].wait()
        grad = matmul(og_ref[...], w_ref[n * half : (n + 1) * half], NT).astype(BF16)
        if n == 0:
            for c in ins[1:]:
                c.wait()
        for i in range(STEP):
            h = n * STEP + i
            lanes = slice(h * DH, (h + 1) * DH)
            owners = slice(h * OWNERS, (h + 1) * OWNERS)
            whole = jnp.concatenate([q_ref[:, lanes], k_ref[:, lanes], v_ref[:, lanes], grad[:, i * DH : (i + 1) * DH]], axis=1)
            for m in range(MOST):
                mask = mask_ref[h, m]
                got = matmul(mask, whole)
                used = jnp.sum(mask.astype(F32), axis=1, keepdims=True)
                rows = slice(m * OWNED, (m + 1) * OWNED)
                for j in range(4):
                    part = got[:, j * DH : (j + 1) * DH]
                    if j == 1:
                        part = part + EMPTY * (1.0 - used)
                    buf_ref[owners, j, rows, :] = part.astype(BF16).reshape(OWNERS, OWNED, DH)
            c = pltpu.make_async_copy(buf_ref.at[pl.ds(h * OWNERS, OWNERS)], out_hbm.at[pl.ds(h * OWNERS, OWNERS)], out_sem.at[h])
            c.start()
            outs.append(c)
    for c in outs:
        c.wait()


def dispatch(core, ids, q, k, v, og, w):
    tok = pltpu.VMEM((TOK, HEADS * DH), BF16)
    return pl.pallas_call(
        dispatch_kernel,
        in_specs=[pl.BlockSpec(memory_space=pltpu.SMEM), VM] + [ANY] * 5,
        out_specs=ANY,
        out_shape=jax.ShapeDtypeStruct((SEQ, 4, ROWS, DH), BF16),
        scratch_shapes=[tok, tok, tok, pltpu.VMEM((TOK, D), BF16), pltpu.VMEM((HEADS * DH, D), BF16), pltpu.VMEM((SEQ, 4, ROWS, DH), BF16),
            pltpu.VMEM((HEADS, MOST, CLUSTERS, TOK), BF16), pltpu.SemaphoreType.DMA((4,)), pltpu.SemaphoreType.DMA((HEADS // STEP,)), pltpu.SemaphoreType.DMA((HEADS,))],
        name="dispatch",
    )(core, ids, q, k, v, og, w)


def masks_kernel(idr_ref, idc_ref, out_ref):
    row, col = idr_ref[0], idc_ref[0]
    t, u = iota((TOK, TOK), 0), iota((TOK, TOK), 1)
    same = jnp.logical_and(col == row, u < t)
    earlier = jnp.max(jnp.where(same, 1, 0), axis=1, keepdims=True)
    slot = (col // OWNED) * ROWS + earlier * OWNED + col % OWNED
    out_ref[0] = jnp.where(iota((TOK, PER_HEAD), 1) == slot, 1.0, 0.0).astype(BF16)


def token_masks(idr, idc):
    return pl.pallas_call(
        masks_kernel,
        grid=(HEADS,),
        in_specs=[
            pl.BlockSpec((1, 1, TOK), lambda h: (h, 0, 0)),
            pl.BlockSpec((1, TOK, 1), lambda h: (h, 0, 0)),
        ],
        out_specs=pl.BlockSpec((1, TOK, PER_HEAD), lambda h: (h, 0, 0)),
        out_shape=jax.ShapeDtypeStruct((HEADS, TOK, PER_HEAD), BF16),
        name="token_masks",
    )(idr, idc)


PB = GROUP * ROWS
PER = GROUP * MOST


def regroup_matrix(inverse):
    a = iota((PB, PB), 1 if inverse else 0)
    b = iota((PB, PB), 0 if inverse else 1)
    want = ((a % PER) // MOST) * ROWS + (a % MOST) * OWNED + a // PER
    return jnp.where(b == want, 1.0, 0.0).astype(BF16)


def each(count, unroll, fn):
    def step(i, carry):
        for n in range(unroll):
            fn(i * unroll + n)
        return carry

    lax.fori_loop(0, count // unroll, step, 0)


def regroup_in(in_ref, targets):
    perm = regroup_matrix(False)
    width = len(targets)
    for s in range(SEQ // GROUP):
        src = slice(s * GROUP, (s + 1) * GROUP)
        dst = slice(s * PER, (s + 1) * PER)
        whole = jnp.concatenate([in_ref[src, j].reshape(PB, DH) for j in range(width)], axis=1)
        got = matmul(perm, whole).astype(BF16)
        for j in range(width):
            targets[j][:, dst, :] = got[:, j * DH : (j + 1) * DH].reshape(OWNED, PER, DH)


def regroup_out(results, out_ref):
    back = regroup_matrix(True)
    for s in range(SEQ // GROUP):
        src = slice(s * GROUP, (s + 1) * GROUP)
        dst = slice(s * PER, (s + 1) * PER)
        whole = jnp.concatenate([r[:, dst, :].reshape(PB, DH) for r in results], axis=1)
        got = matmul(back, whole).astype(BF16)
        for j in range(len(results)):
            out_ref[src, j] = got[:, j * DH : (j + 1) * DH].reshape(GROUP, ROWS, DH)


def probabilities(q, k):
    causal = iota((SLOTS, SLOTS), 0) <= iota((SLOTS, SLOTS), 1)
    scores = matmul(k, q, NT) * SCALE
    allowed = jnp.logical_and(causal, k[:, 0:1].astype(F32) < 0.5 * EMPTY)
    scores = jnp.where(allowed, scores, NEGATIVE)
    weights = jnp.exp(scores - jnp.max(scores, axis=0, keepdims=True))
    return weights * (1.0 / jnp.sum(weights, axis=0, keepdims=True))


GROUPED = (OWNED, SLOTS, DH)


def load_parts(in_hbm, buf, sem, js):
    each_src = SEQ // PARTS
    cs = []
    for n in range(PARTS):
        src = pl.ds(n * each_src, each_src)
        c = pltpu.make_async_copy(in_hbm.at[src, js], buf.at[src], sem.at[n])
        c.start(); cs.append(c)
    return cs

def forward_kernel(in_hbm, out_ref, buf_ref, q_ref, k_ref, v_ref, o_ref, sem):
    cs = load_parts(in_hbm, buf_ref, sem, pl.ds(0, 3))
    perm = regroup_matrix(False)
    per = SEQ // GROUP // PARTS
    targets = (q_ref, k_ref, v_ref)
    for s in range(SEQ // GROUP):
        if s % per == 0:
            cs[s // per].wait()
        src = slice(s * GROUP, (s + 1) * GROUP)
        dst = slice(s * PER, (s + 1) * PER)
        whole = jnp.concatenate([buf_ref[src, j].reshape(PB, DH) for j in range(3)], axis=1)
        got = matmul(perm, whole).astype(BF16)
        for j in range(3):
            targets[j][:, dst, :] = got[:, j * DH : (j + 1) * DH].reshape(OWNED, PER, DH)
    def one(c):
        half = probabilities(q_ref[c], k_ref[c]).astype(BF16)
        o_ref[c] = matmul(half, v_ref[c], TN).astype(BF16)
    each(OWNED, 16, one)
    regroup_out((o_ref,), out_ref)


def forward(received):
    return pl.pallas_call(
        forward_kernel,
        in_specs=[ANY],
        out_specs=VM,
        out_shape=jax.ShapeDtypeStruct((SEQ, 1, ROWS, DH), BF16),
        scratch_shapes=[pltpu.VMEM((SEQ, 3, ROWS, DH), BF16)] + [pltpu.VMEM(GROUPED, BF16)] * 4 + [pltpu.SemaphoreType.DMA((PARTS,))],
        name="cluster_forward",
    )(received)


def backward_kernel(in_ref, out_ref, q_ref, k_ref, v_ref, g_ref, dq_ref, dk_ref, dv_ref):
    regroup_in(in_ref, (q_ref, k_ref, v_ref, g_ref))
    def one(c):
        q, k, v, g = q_ref[c], k_ref[c], v_ref[c], g_ref[c]
        probs = probabilities(q, k)
        dprob = matmul(v, g, NT)
        delta = jnp.sum(probs * dprob, axis=0, keepdims=True)
        ds = (probs * (dprob - delta)).astype(BF16)
        dv_ref[c] = matmul(probs.astype(BF16), g).astype(BF16)
        dk_ref[c] = (matmul(ds, q) * SCALE).astype(BF16)
        dq_ref[c] = (matmul(ds, k, TN) * SCALE).astype(BF16)
    each(OWNED, 8, one)
    regroup_out((dq_ref, dk_ref, dv_ref), out_ref)


def backward(received):
    return pl.pallas_call(
        backward_kernel,
        in_specs=[VM],
        out_specs=VM,
        out_shape=jax.ShapeDtypeStruct((SEQ, 3, ROWS, DH), BF16),
        scratch_shapes=[pltpu.VMEM(GROUPED, BF16)] * 7,
        name="cluster_backward",
    )(received)


def attn_kernel(core_ref, mask_ref, in_ref, w_ref, attn_ref, other_ref, acc_ref):
    h = pl.program_id(0)
    for i in range(PAIR):
        owners = pl.ds((h * PAIR + i) * OWNERS, OWNERS)
        rows = in_ref[owners, 0].reshape(PER_HEAD, DH)
        attn_ref[:, i * DH : (i + 1) * DH] = matmul(mask_ref[i], rows).astype(BF16)
    part = matmul(attn_ref[...], w_ref[...])

    @pl.when(h == 0)
    def _():
        acc_ref[...] = part

    @pl.when(h > 0)
    def _():
        acc_ref[...] += part

    @pl.when(h == HEADS // PAIR - 1)
    def _():
        other_ref[...] = acc_ref[...].astype(BF16)


def attn_combine(core, masks, received, weight):
    return pl.pallas_call(
        attn_kernel,
        grid_spec=pltpu.PrefetchScalarGridSpec(
            num_scalar_prefetch=1,
            grid=(HEADS // PAIR,),
            in_specs=[
                pl.BlockSpec((PAIR, TOK, PER_HEAD), lambda h, core: (h, 0, 0)),
                VM,
                pl.BlockSpec((PAIR * DH, D // 2), lambda h, core: (h, 1 - core[0])),
            ],
            out_specs=[
                pl.BlockSpec((TOK, PAIR * DH), lambda h, core: (0, h)),
                pl.BlockSpec((TOK, D // 2), lambda h, core: (0, 0)),
            ],
            scratch_shapes=[pltpu.VMEM((TOK, D // 2), F32)],
        ),
        out_shape=[
            jax.ShapeDtypeStruct((TOK, HEADS * DH), BF16),
            jax.ShapeDtypeStruct((TOK, D // 2), BF16),
        ],
        name="attn_combine",
    )(core, masks, received, weight)


def grads_kernel(mask_hbm, in_hbm, dq_hbm, dk_hbm, dv_hbm, mask_ref, buf_ref, out_ref, in_sem, out_sem):
    outs = (dq_hbm, dk_hbm, dv_hbm)
    ins = []
    for h in range(HEADS):
        owners = pl.ds(h * OWNERS, OWNERS)
        a = pltpu.make_async_copy(mask_hbm.at[h], mask_ref.at[h], in_sem.at[h, 0])
        b = pltpu.make_async_copy(in_hbm.at[owners], buf_ref.at[owners], in_sem.at[h, 1])
        a.start()
        b.start()
        ins.append((a, b))
    sent = []
    for h in range(HEADS):
        for c in ins[h]:
            c.wait()
        owners = slice(h * OWNERS, (h + 1) * OWNERS)
        whole = jnp.concatenate([buf_ref[owners, j].reshape(PER_HEAD, DH) for j in range(3)], axis=1)
        got = matmul(mask_ref[h], whole).astype(BF16)
        for j in range(3):
            out_ref[j, :, h * DH : (h + 1) * DH] = got[:, j * DH : (j + 1) * DH]
        if h % PAIR == PAIR - 1:
            n = h // PAIR
            lanes = pl.ds(n * PAIR * DH, PAIR * DH)
            for j in range(3):
                c = pltpu.make_async_copy(out_ref.at[j, :, lanes], outs[j].at[:, lanes], out_sem.at[n, j])
                c.start()
                sent.append(c)
    for c in sent:
        c.wait()


def grads_combine(masks, received):
    return pl.pallas_call(
        grads_kernel,
        in_specs=[ANY] * 2,
        out_specs=[ANY] * 3,
        out_shape=[jax.ShapeDtypeStruct((TOK, HEADS * DH), BF16)] * 3,
        scratch_shapes=[
            pltpu.VMEM((HEADS, TOK, PER_HEAD), BF16),
            pltpu.VMEM((SEQ, 3, ROWS, DH), BF16),
            pltpu.VMEM((3, TOK, HEADS * DH), BF16),
            pltpu.SemaphoreType.DMA((HEADS, 2)),
            pltpu.SemaphoreType.DMA((HEADS // PAIR, 3)),
        ],
        name="grads_combine",
    )(masks, received)


def own_half_kernel(core_ref, attn_ref, w_ref, came_ref, out_ref):
    mine = matmul(attn_ref[...], w_ref[...])
    out_ref[...] = (mine + came_ref[...].astype(F32)).astype(BF16)


def own_half(core, attn, weight, came):
    width = 256
    steps = D // 2 // width
    return pl.pallas_call(
        own_half_kernel,
        grid_spec=pltpu.PrefetchScalarGridSpec(
            num_scalar_prefetch=1,
            grid=(steps,),
            in_specs=[
                pl.BlockSpec((TOK, HEADS * DH), lambda n, core: (0, 0)),
                pl.BlockSpec((HEADS * DH, width), lambda n, core: (0, core[0] * steps + n)),
                pl.BlockSpec((TOK, width), lambda n, core: (0, n)),
            ],
            out_specs=pl.BlockSpec((TOK, width), lambda n, core: (0, n)),
        ),
        out_shape=jax.ShapeDtypeStruct((TOK, D // 2), BF16),
        name="own_half",
    )(core, attn, weight, came)


def exchange(x):
    return lax.all_to_all(x, "seq", split_axis=0, concat_axis=0, tiled=True)


def in_vmem(x):
    return pltpu.with_memory_space_constraint(x, pltpu.MemorySpace.VMEM)


def body(query_rows, key_rows, value_rows, out_grad, cluster_ids, out_weight):
    idr = jnp.transpose(cluster_ids, (0, 2, 1))
    core = lax.axis_index("head").astype(jnp.int32).reshape(1)
    masks = token_masks(idr, cluster_ids)
    received = exchange(dispatch(core, idr, query_rows, key_rows, value_rows, out_grad, out_weight))
    attn_back = in_vmem(exchange(forward(received)))
    back = exchange(backward(received))
    attn, other = attn_combine(core, masks, attn_back, out_weight)
    came = lax.ppermute(other, "head", [(0, 1), (1, 0)])
    layer_out = own_half(core, attn, out_weight, came)
    dq, dk, dv = grads_combine(masks, back)
    return layer_out, dq, dk, dv


def solution(mesh):
    in_specs = (
        P("seq", "head"),
        P("seq", "head"),
        P("seq", "head"),
        P("seq", None),
        P("head", "seq", None),
        P("head", None),
    )
    out_specs = (P("seq", "head"), P("seq", "head"), P("seq", "head"), P("seq", "head"))
    return jax.shard_map(body, mesh=mesh, in_specs=in_specs, out_specs=out_specs, check_vma=False)
```

```python
import jax
import jax.numpy as jnp
from jax import lax
from jax.experimental import pallas as pl
from jax.experimental.pallas import tpu as pltpu
from jax.sharding import PartitionSpec as P

CLUSTERS = 256
MOST = 2
DH = 128
SEQ = 128
HEADS = 8
TOK = 384
D = 2048
PER_HEAD = CLUSTERS * MOST
OWNERS = SEQ // HEADS
OWNED = CLUSTERS // OWNERS
ROWS = OWNED * MOST
SLOTS = SEQ * MOST
GROUP = 8
PAIR = 2
STEP = 4
STAGGER_NS = 45000
EMPTY = 64.0
NEGATIVE = -1e30
SCALE = DH ** -0.5
F32 = jnp.float32
BF16 = jnp.bfloat16

VM = pl.BlockSpec(memory_space=pltpu.VMEM)
ANY = pl.BlockSpec(memory_space=pl.ANY)

NT = ((1,), (1,))
NN = ((1,), (0,))
TN = ((0,), (0,))


def matmul(a, b, dims=NN):
    return lax.dot_general(a, b, (dims, ((), ())), preferred_element_type=F32)


def iota(shape, dim):
    return lax.broadcasted_iota(jnp.int32, shape, dim)


def send_masks(ids):
    before = jnp.where(iota((TOK, TOK), 0) < iota((TOK, TOK), 1), 1.0, 0.0).astype(BF16)
    hit = jnp.where(iota((CLUSTERS, TOK), 0) == ids, 1.0, 0.0)
    earlier = matmul(hit.astype(BF16), before)
    return [jnp.where(earlier == m, hit, 0.0) for m in range(MOST)]


def dispatch_kernel(core_ref, ids_ref, q_hbm, k_hbm, v_hbm, og_hbm, w_hbm, out_hbm, q_ref, k_ref, v_ref, og_ref, w_ref, buf_ref, mask_ref, in_sem, w_sem, out_sem):
    half = STEP * DH
    ins = [pltpu.make_async_copy(a, b, in_sem.at[i]) for i, (a, b) in enumerate(((og_hbm, og_ref), (q_hbm, q_ref), (k_hbm, k_ref), (v_hbm, v_ref)))]
    ws = [pltpu.make_async_copy(w_hbm.at[pl.ds(n * half, half)], w_ref.at[pl.ds(n * half, half)], w_sem.at[n]) for n in range(HEADS // STEP)]
    ins[0].start()
    ws[0].start()
    for c in ins[1:]:
        c.start()
    for c in ws[1:]:
        c.start()

    @pl.when(core_ref[0] == 1)
    def _():
        pl.delay(STAGGER_NS)

    for h in range(HEADS):
        for m, mask in enumerate(send_masks(ids_ref[h])):
            mask_ref[h, m] = mask.astype(BF16)
    ins[0].wait()
    outs = []
    for n in range(HEADS // STEP):
        ws[n].wait()
        grad = matmul(og_ref[...], w_ref[n * half : (n + 1) * half], NT).astype(BF16)
        if n == 0:
            for c in ins[1:]:
                c.wait()
        for i in range(STEP):
            h = n * STEP + i
            lanes = slice(h * DH, (h + 1) * DH)
            owners = slice(h * OWNERS, (h + 1) * OWNERS)
            whole = jnp.concatenate([q_ref[:, lanes], k_ref[:, lanes], v_ref[:, lanes], grad[:, i * DH : (i + 1) * DH]], axis=1)
            for m in range(MOST):
                mask = mask_ref[h, m]
                got = matmul(mask, whole)
                used = jnp.sum(mask.astype(F32), axis=1, keepdims=True)
                rows = slice(m * OWNED, (m + 1) * OWNED)
                for j in range(4):
                    part = got[:, j * DH : (j + 1) * DH]
                    if j == 1:
                        part = part + EMPTY * (1.0 - used)
                    buf_ref[owners, j, rows, :] = part.astype(BF16).reshape(OWNERS, OWNED, DH)
            c = pltpu.make_async_copy(buf_ref.at[pl.ds(h * OWNERS, OWNERS)], out_hbm.at[pl.ds(h * OWNERS, OWNERS)], out_sem.at[h])
            c.start()
            outs.append(c)
    for c in outs:
        c.wait()


def dispatch(core, ids, q, k, v, og, w):
    tok = pltpu.VMEM((TOK, HEADS * DH), BF16)
    return pl.pallas_call(
        dispatch_kernel,
        in_specs=[pl.BlockSpec(memory_space=pltpu.SMEM), VM] + [ANY] * 5,
        out_specs=ANY,
        out_shape=jax.ShapeDtypeStruct((SEQ, 4, ROWS, DH), BF16),
        scratch_shapes=[tok, tok, tok, pltpu.VMEM((TOK, D), BF16), pltpu.VMEM((HEADS * DH, D), BF16), pltpu.VMEM((SEQ, 4, ROWS, DH), BF16),
            pltpu.VMEM((HEADS, MOST, CLUSTERS, TOK), BF16), pltpu.SemaphoreType.DMA((4,)), pltpu.SemaphoreType.DMA((HEADS // STEP,)), pltpu.SemaphoreType.DMA((HEADS,))],
        name="dispatch",
    )(core, ids, q, k, v, og, w)


def masks_kernel(idr_ref, idc_ref, out_ref):
    row, col = idr_ref[0], idc_ref[0]
    t, u = iota((TOK, TOK), 0), iota((TOK, TOK), 1)
    same = jnp.logical_and(col == row, u < t)
    earlier = jnp.max(jnp.where(same, 1, 0), axis=1, keepdims=True)
    slot = (col // OWNED) * ROWS + earlier * OWNED + col % OWNED
    out_ref[0] = jnp.where(iota((TOK, PER_HEAD), 1) == slot, 1.0, 0.0).astype(BF16)


def token_masks(idr, idc):
    return pl.pallas_call(
        masks_kernel,
        grid=(HEADS,),
        in_specs=[
            pl.BlockSpec((1, 1, TOK), lambda h: (h, 0, 0)),
            pl.BlockSpec((1, TOK, 1), lambda h: (h, 0, 0)),
        ],
        out_specs=pl.BlockSpec((1, TOK, PER_HEAD), lambda h: (h, 0, 0)),
        out_shape=jax.ShapeDtypeStruct((HEADS, TOK, PER_HEAD), BF16),
        name="token_masks",
    )(idr, idc)


PB = GROUP * ROWS
PER = GROUP * MOST


def regroup_matrix(inverse):
    a = iota((PB, PB), 1 if inverse else 0)
    b = iota((PB, PB), 0 if inverse else 1)
    want = ((a % PER) // MOST) * ROWS + (a % MOST) * OWNED + a // PER
    return jnp.where(b == want, 1.0, 0.0).astype(BF16)


def each(count, unroll, fn):
    def step(i, carry):
        for n in range(unroll):
            fn(i * unroll + n)
        return carry

    lax.fori_loop(0, count // unroll, step, 0)


def regroup_in(in_ref, targets):
    perm = regroup_matrix(False)
    width = len(targets)
    for s in range(SEQ // GROUP):
        src = slice(s * GROUP, (s + 1) * GROUP)
        dst = slice(s * PER, (s + 1) * PER)
        whole = jnp.concatenate([in_ref[src, j].reshape(PB, DH) for j in range(width)], axis=1)
        got = matmul(perm, whole).astype(BF16)
        for j in range(width):
            targets[j][:, dst, :] = got[:, j * DH : (j + 1) * DH].reshape(OWNED, PER, DH)


def regroup_out(results, out_ref):
    back = regroup_matrix(True)
    for s in range(SEQ // GROUP):
        src = slice(s * GROUP, (s + 1) * GROUP)
        dst = slice(s * PER, (s + 1) * PER)
        whole = jnp.concatenate([r[:, dst, :].reshape(PB, DH) for r in results], axis=1)
        got = matmul(back, whole).astype(BF16)
        for j in range(len(results)):
            out_ref[src, j] = got[:, j * DH : (j + 1) * DH].reshape(GROUP, ROWS, DH)


def probabilities(q, k):
    causal = iota((SLOTS, SLOTS), 0) <= iota((SLOTS, SLOTS), 1)
    scores = matmul(k, q, NT) * SCALE
    allowed = jnp.logical_and(causal, k[:, 0:1].astype(F32) < 0.5 * EMPTY)
    scores = jnp.where(allowed, scores, NEGATIVE)
    weights = jnp.exp(scores - jnp.max(scores, axis=0, keepdims=True))
    return weights * (1.0 / jnp.sum(weights, axis=0, keepdims=True))


GROUPED = (OWNED, SLOTS, DH)


def owner_kernel(in_ref, out_ref, q_ref, k_ref, v_ref, g_ref, o_ref, dq_ref, dk_ref, dv_ref):
    regroup_in(in_ref, (q_ref, k_ref, v_ref, g_ref))

    def one(c):
        q, k, v, g = q_ref[c], k_ref[c], v_ref[c], g_ref[c]
        probs = probabilities(q, k)
        half = probs.astype(BF16)
        dprob = matmul(v, g, NT)
        delta = jnp.sum(probs * dprob, axis=0, keepdims=True)
        ds = (probs * (dprob - delta)).astype(BF16)
        o_ref[c] = matmul(half, v, TN).astype(BF16)
        dv_ref[c] = matmul(half, g).astype(BF16)
        dk_ref[c] = (matmul(ds, q) * SCALE).astype(BF16)
        dq_ref[c] = (matmul(ds, k, TN) * SCALE).astype(BF16)

    each(OWNED, 8, one)
    regroup_out((o_ref, dq_ref, dk_ref, dv_ref), out_ref)


def owner(received):
    return pl.pallas_call(
        owner_kernel,
        in_specs=[VM],
        out_specs=VM,
        out_shape=jax.ShapeDtypeStruct((SEQ, 4, ROWS, DH), BF16),
        scratch_shapes=[pltpu.VMEM(GROUPED, BF16)] * 8,
        name="owner",
    )(received)


def attn_kernel(core_ref, mask_ref, in_ref, w_ref, attn_ref, other_ref, acc_ref):
    h = pl.program_id(0)
    for i in range(PAIR):
        rows = in_ref[i * OWNERS : (i + 1) * OWNERS, 0].reshape(PER_HEAD, DH)
        attn_ref[:, i * DH : (i + 1) * DH] = matmul(mask_ref[i], rows).astype(BF16)
    part = matmul(attn_ref[...], w_ref[...])

    @pl.when(h == 0)
    def _():
        acc_ref[...] = part

    @pl.when(h > 0)
    def _():
        acc_ref[...] += part

    @pl.when(h == HEADS // PAIR - 1)
    def _():
        other_ref[...] = acc_ref[...].astype(BF16)


def attn_combine(core, masks, received, weight):
    return pl.pallas_call(
        attn_kernel,
        grid_spec=pltpu.PrefetchScalarGridSpec(
            num_scalar_prefetch=1,
            grid=(HEADS // PAIR,),
            in_specs=[
                pl.BlockSpec((PAIR, TOK, PER_HEAD), lambda h, core: (h, 0, 0)),
                pl.BlockSpec((PAIR * OWNERS, 1, ROWS, DH), lambda h, core: (h, 0, 0, 0)),
                pl.BlockSpec((PAIR * DH, D // 2), lambda h, core: (h, 1 - core[0])),
            ],
            out_specs=[
                pl.BlockSpec((TOK, PAIR * DH), lambda h, core: (0, h)),
                pl.BlockSpec((TOK, D // 2), lambda h, core: (0, 0)),
            ],
            scratch_shapes=[pltpu.VMEM((TOK, D // 2), F32)],
        ),
        out_shape=[
            jax.ShapeDtypeStruct((TOK, HEADS * DH), BF16),
            jax.ShapeDtypeStruct((TOK, D // 2), BF16),
        ],
        name="attn_combine",
    )(core, masks, received, weight)


def grads_kernel(mask_hbm, in_hbm, dq_hbm, dk_hbm, dv_hbm, mask_ref, buf_ref, out_ref, in_sem, out_sem):
    outs = (dq_hbm, dk_hbm, dv_hbm)
    ins = []
    for h in range(HEADS):
        owners = pl.ds(h * OWNERS, OWNERS)
        a = pltpu.make_async_copy(mask_hbm.at[h], mask_ref.at[h], in_sem.at[h, 0])
        b = pltpu.make_async_copy(in_hbm.at[owners, pl.ds(1, 3)], buf_ref.at[owners], in_sem.at[h, 1])
        a.start()
        b.start()
        ins.append((a, b))
    sent = []
    for h in range(HEADS):
        for c in ins[h]:
            c.wait()
        owners = slice(h * OWNERS, (h + 1) * OWNERS)
        whole = jnp.concatenate([buf_ref[owners, j].reshape(PER_HEAD, DH) for j in range(3)], axis=1)
        got = matmul(mask_ref[h], whole).astype(BF16)
        for j in range(3):
            out_ref[j, :, h * DH : (h + 1) * DH] = got[:, j * DH : (j + 1) * DH]
        if h % PAIR == PAIR - 1:
            n = h // PAIR
            lanes = pl.ds(n * PAIR * DH, PAIR * DH)
            for j in range(3):
                c = pltpu.make_async_copy(out_ref.at[j, :, lanes], outs[j].at[:, lanes], out_sem.at[n, j])
                c.start()
                sent.append(c)
    for c in sent:
        c.wait()


def grads_combine(masks, received):
    return pl.pallas_call(
        grads_kernel,
        in_specs=[ANY] * 2,
        out_specs=[ANY] * 3,
        out_shape=[jax.ShapeDtypeStruct((TOK, HEADS * DH), BF16)] * 3,
        scratch_shapes=[
            pltpu.VMEM((HEADS, TOK, PER_HEAD), BF16),
            pltpu.VMEM((SEQ, 3, ROWS, DH), BF16),
            pltpu.VMEM((3, TOK, HEADS * DH), BF16),
            pltpu.SemaphoreType.DMA((HEADS, 2)),
            pltpu.SemaphoreType.DMA((HEADS // PAIR, 3)),
        ],
        name="grads_combine",
    )(masks, received)


def own_half_kernel(core_ref, attn_ref, w_ref, came_ref, out_ref):
    mine = matmul(attn_ref[...], w_ref[...])
    out_ref[...] = (mine + came_ref[...].astype(F32)).astype(BF16)


def own_half(core, attn, weight, came):
    width = 256
    steps = D // 2 // width
    return pl.pallas_call(
        own_half_kernel,
        grid_spec=pltpu.PrefetchScalarGridSpec(
            num_scalar_prefetch=1,
            grid=(steps,),
            in_specs=[
                pl.BlockSpec((TOK, HEADS * DH), lambda n, core: (0, 0)),
                pl.BlockSpec((HEADS * DH, width), lambda n, core: (0, core[0] * steps + n)),
                pl.BlockSpec((TOK, width), lambda n, core: (0, n)),
            ],
            out_specs=pl.BlockSpec((TOK, width), lambda n, core: (0, n)),
        ),
        out_shape=jax.ShapeDtypeStruct((TOK, D // 2), BF16),
        name="own_half",
    )(core, attn, weight, came)


def exchange(x):
    return lax.all_to_all(x, "seq", split_axis=0, concat_axis=0, tiled=True)


def body(query_rows, key_rows, value_rows, out_grad, cluster_ids, out_weight):
    idr = jnp.transpose(cluster_ids, (0, 2, 1))
    core = lax.axis_index("head").astype(jnp.int32).reshape(1)
    masks = token_masks(idr, cluster_ids)
    received = exchange(dispatch(core, idr, query_rows, key_rows, value_rows, out_grad, out_weight))
    back = exchange(owner(received))
    attn, other = attn_combine(core, masks, back, out_weight)
    came = lax.ppermute(other, "head", [(0, 1), (1, 0)])
    layer_out = own_half(core, attn, out_weight, came)
    dq, dk, dv = grads_combine(masks, back)
    return layer_out, dq, dk, dv


def solution(mesh):
    in_specs = (
        P("seq", "head"),
        P("seq", "head"),
        P("seq", "head"),
        P("seq", None),
        P("head", "seq", None),
        P("head", None),
    )
    out_specs = (P("seq", "head"), P("seq", "head"), P("seq", "head"), P("seq", "head"))
    return jax.shard_map(body, mesh=mesh, in_specs=in_specs, out_specs=out_specs, check_vma=False)
```

```python
import jax
import jax.numpy as jnp
from jax import lax
from jax.experimental import pallas as pl
from jax.experimental.pallas import tpu as pltpu
from jax.sharding import PartitionSpec as P

CLUSTERS = 256
MOST = 2
DH = 128
SEQ = 128
HEADS = 8
TOK = 384
D = 2048
PER_HEAD = CLUSTERS * MOST
OWNERS = SEQ // HEADS
OWNED = CLUSTERS // OWNERS
ROWS = OWNED * MOST
SLOTS = SEQ * MOST
GROUP = 8
PAIR = 2
STEP = 4
PARTS = 4
STAGGER_NS = 28000
EMPTY = 64.0
NEGATIVE = -1e30
SCALE = DH ** -0.5
F32 = jnp.float32
BF16 = jnp.bfloat16

VM = pl.BlockSpec(memory_space=pltpu.VMEM)
ANY = pl.BlockSpec(memory_space=pl.ANY)

NT = ((1,), (1,))
NN = ((1,), (0,))
TN = ((0,), (0,))


def matmul(a, b, dims=NN):
    return lax.dot_general(a, b, (dims, ((), ())), preferred_element_type=F32)


def iota(shape, dim):
    return lax.broadcasted_iota(jnp.int32, shape, dim)


def send_masks(ids):
    before = jnp.where(iota((TOK, TOK), 0) < iota((TOK, TOK), 1), 1.0, 0.0).astype(BF16)
    hit = jnp.where(iota((CLUSTERS, TOK), 0) == ids, 1.0, 0.0)
    earlier = matmul(hit.astype(BF16), before)
    return [jnp.where(earlier == m, hit, 0.0) for m in range(MOST)]


def dispatch_kernel(core_ref, ids_ref, q_hbm, k_hbm, v_hbm, og_hbm, w_hbm, out_hbm, q_ref, k_ref, v_ref, og_ref, w_ref, buf_ref, mask_ref, in_sem, w_sem, out_sem):
    half = STEP * DH
    ins = [pltpu.make_async_copy(a, b, in_sem.at[i]) for i, (a, b) in enumerate(((og_hbm, og_ref), (q_hbm, q_ref), (k_hbm, k_ref), (v_hbm, v_ref)))]
    ws = [pltpu.make_async_copy(w_hbm.at[pl.ds(n * half, half)], w_ref.at[pl.ds(n * half, half)], w_sem.at[n]) for n in range(HEADS // STEP)]
    ins[0].start()
    ws[0].start()
    for c in ins[1:]:
        c.start()
    for c in ws[1:]:
        c.start()

    @pl.when(core_ref[0] == 1)
    def _():
        pl.delay(STAGGER_NS)

    for h in range(HEADS):
        for m, mask in enumerate(send_masks(ids_ref[h])):
            mask_ref[h, m] = mask.astype(BF16)
    ins[0].wait()
    outs = []
    for n in range(HEADS // STEP):
        ws[n].wait()
        grad = matmul(og_ref[...], w_ref[n * half : (n + 1) * half], NT).astype(BF16)
        if n == 0:
            for c in ins[1:]:
                c.wait()
        for i in range(STEP):
            h = n * STEP + i
            lanes = slice(h * DH, (h + 1) * DH)
            owners = slice(h * OWNERS, (h + 1) * OWNERS)
            whole = jnp.concatenate([q_ref[:, lanes], k_ref[:, lanes], v_ref[:, lanes], grad[:, i * DH : (i + 1) * DH]], axis=1)
            for m in range(MOST):
                mask = mask_ref[h, m]
                got = matmul(mask, whole)
                used = jnp.sum(mask.astype(F32), axis=1, keepdims=True)
                rows = slice(m * OWNED, (m + 1) * OWNED)
                for j in range(4):
                    part = got[:, j * DH : (j + 1) * DH]
                    if j == 1:
                        part = part + EMPTY * (1.0 - used)
                    buf_ref[owners, j, rows, :] = part.astype(BF16).reshape(OWNERS, OWNED, DH)
            c = pltpu.make_async_copy(buf_ref.at[pl.ds(h * OWNERS, OWNERS)], out_hbm.at[pl.ds(h * OWNERS, OWNERS)], out_sem.at[h])
            c.start()
            outs.append(c)
    for c in outs:
        c.wait()


def dispatch(core, ids, q, k, v, og, w):
    tok = pltpu.VMEM((TOK, HEADS * DH), BF16)
    return pl.pallas_call(
        dispatch_kernel,
        in_specs=[pl.BlockSpec(memory_space=pltpu.SMEM), VM] + [ANY] * 5,
        out_specs=ANY,
        out_shape=jax.ShapeDtypeStruct((SEQ, 4, ROWS, DH), BF16),
        scratch_shapes=[tok, tok, tok, pltpu.VMEM((TOK, D), BF16), pltpu.VMEM((HEADS * DH, D), BF16), pltpu.VMEM((SEQ, 4, ROWS, DH), BF16),
            pltpu.VMEM((HEADS, MOST, CLUSTERS, TOK), BF16), pltpu.SemaphoreType.DMA((4,)), pltpu.SemaphoreType.DMA((HEADS // STEP,)), pltpu.SemaphoreType.DMA((HEADS,))],
        name="dispatch",
    )(core, ids, q, k, v, og, w)


def masks_kernel(idr_ref, idc_ref, out_ref):
    row, col = idr_ref[0], idc_ref[0]
    t, u = iota((TOK, TOK), 0), iota((TOK, TOK), 1)
    same = jnp.logical_and(col == row, u < t)
    earlier = jnp.max(jnp.where(same, 1, 0), axis=1, keepdims=True)
    slot = (col // OWNED) * ROWS + earlier * OWNED + col % OWNED
    out_ref[0] = jnp.where(iota((TOK, PER_HEAD), 1) == slot, 1.0, 0.0).astype(BF16)


def token_masks(idr, idc):
    return pl.pallas_call(
        masks_kernel,
        grid=(HEADS,),
        in_specs=[
            pl.BlockSpec((1, 1, TOK), lambda h: (h, 0, 0)),
            pl.BlockSpec((1, TOK, 1), lambda h: (h, 0, 0)),
        ],
        out_specs=pl.BlockSpec((1, TOK, PER_HEAD), lambda h: (h, 0, 0)),
        out_shape=jax.ShapeDtypeStruct((HEADS, TOK, PER_HEAD), BF16),
        name="token_masks",
    )(idr, idc)


PB = GROUP * ROWS
PER = GROUP * MOST


def regroup_matrix(inverse):
    a = iota((PB, PB), 1 if inverse else 0)
    b = iota((PB, PB), 0 if inverse else 1)
    want = ((a % PER) // MOST) * ROWS + (a % MOST) * OWNED + a // PER
    return jnp.where(b == want, 1.0, 0.0).astype(BF16)


def each(count, unroll, fn):
    def step(i, carry):
        for n in range(unroll):
            fn(i * unroll + n)
        return carry

    lax.fori_loop(0, count // unroll, step, 0)


def regroup_in(in_ref, targets):
    perm = regroup_matrix(False)
    width = len(targets)
    for s in range(SEQ // GROUP):
        src = slice(s * GROUP, (s + 1) * GROUP)
        dst = slice(s * PER, (s + 1) * PER)
        whole = jnp.concatenate([in_ref[src, j].reshape(PB, DH) for j in range(width)], axis=1)
        got = matmul(perm, whole).astype(BF16)
        for j in range(width):
            targets[j][:, dst, :] = got[:, j * DH : (j + 1) * DH].reshape(OWNED, PER, DH)


def regroup_out(results, out_ref):
    back = regroup_matrix(True)
    for s in range(SEQ // GROUP):
        src = slice(s * GROUP, (s + 1) * GROUP)
        dst = slice(s * PER, (s + 1) * PER)
        whole = jnp.concatenate([r[:, dst, :].reshape(PB, DH) for r in results], axis=1)
        got = matmul(back, whole).astype(BF16)
        for j in range(len(results)):
            out_ref[src, j] = got[:, j * DH : (j + 1) * DH].reshape(GROUP, ROWS, DH)


def probabilities(q, k):
    causal = iota((SLOTS, SLOTS), 0) <= iota((SLOTS, SLOTS), 1)
    scores = matmul(k, q, NT) * SCALE
    allowed = jnp.logical_and(causal, k[:, 0:1].astype(F32) < 0.5 * EMPTY)
    scores = jnp.where(allowed, scores, NEGATIVE)
    weights = jnp.exp(scores - jnp.max(scores, axis=0, keepdims=True))
    return weights * (1.0 / jnp.sum(weights, axis=0, keepdims=True))


GROUPED = (OWNED, SLOTS, DH)


def load_parts(in_hbm, buf, sem, js):
    each_src = SEQ // PARTS
    cs = []
    for n in range(PARTS):
        src = pl.ds(n * each_src, each_src)
        c = pltpu.make_async_copy(in_hbm.at[src, js], buf.at[src], sem.at[n])
        c.start(); cs.append(c)
    return cs

def forward_kernel(in_hbm, out_ref, buf_ref, q_ref, k_ref, v_ref, o_ref, sem):
    cs = load_parts(in_hbm, buf_ref, sem, pl.ds(0, 3))
    perm = regroup_matrix(False)
    per = SEQ // GROUP // PARTS
    targets = (q_ref, k_ref, v_ref)
    for s in range(SEQ // GROUP):
        if s % per == 0:
            cs[s // per].wait()
        src = slice(s * GROUP, (s + 1) * GROUP)
        dst = slice(s * PER, (s + 1) * PER)
        whole = jnp.concatenate([buf_ref[src, j].reshape(PB, DH) for j in range(3)], axis=1)
        got = matmul(perm, whole).astype(BF16)
        for j in range(3):
            targets[j][:, dst, :] = got[:, j * DH : (j + 1) * DH].reshape(OWNED, PER, DH)
    def one(c):
        half = probabilities(q_ref[c], k_ref[c]).astype(BF16)
        o_ref[c] = matmul(half, v_ref[c], TN).astype(BF16)
    each(OWNED, 16, one)
    regroup_out((o_ref,), out_ref)


def forward(received):
    return pl.pallas_call(
        forward_kernel,
        in_specs=[ANY],
        out_specs=VM,
        out_shape=jax.ShapeDtypeStruct((SEQ, 1, ROWS, DH), BF16),
        scratch_shapes=[pltpu.VMEM((SEQ, 3, ROWS, DH), BF16)] + [pltpu.VMEM(GROUPED, BF16)] * 4 + [pltpu.SemaphoreType.DMA((PARTS,))],
        name="cluster_forward",
    )(received)


def backward_kernel(in_ref, out_ref, q_ref, k_ref, v_ref, g_ref, dq_ref, dk_ref, dv_ref):
    regroup_in(in_ref, (q_ref, k_ref, v_ref, g_ref))
    def one(c):
        q, k, v, g = q_ref[c], k_ref[c], v_ref[c], g_ref[c]
        probs = probabilities(q, k)
        dprob = matmul(v, g, NT)
        delta = jnp.sum(probs * dprob, axis=0, keepdims=True)
        ds = (probs * (dprob - delta)).astype(BF16)
        dv_ref[c] = matmul(probs.astype(BF16), g).astype(BF16)
        dk_ref[c] = (matmul(ds, q) * SCALE).astype(BF16)
        dq_ref[c] = (matmul(ds, k, TN) * SCALE).astype(BF16)
    each(OWNED, 8, one)
    regroup_out((dq_ref, dk_ref, dv_ref), out_ref)


def backward(received):
    return pl.pallas_call(
        backward_kernel,
        in_specs=[VM],
        out_specs=VM,
        out_shape=jax.ShapeDtypeStruct((SEQ, 3, ROWS, DH), BF16),
        scratch_shapes=[pltpu.VMEM(GROUPED, BF16)] * 7,
        name="cluster_backward",
    )(received)


def attn_kernel(core_ref, mask_ref, in_ref, w_ref, attn_ref, other_ref, acc_ref):
    h = pl.program_id(0)
    for i in range(PAIR):
        owners = pl.ds((h * PAIR + i) * OWNERS, OWNERS)
        rows = in_ref[owners, 0].reshape(PER_HEAD, DH)
        attn_ref[:, i * DH : (i + 1) * DH] = matmul(mask_ref[i], rows).astype(BF16)
    part = matmul(attn_ref[...], w_ref[...])

    @pl.when(h == 0)
    def _():
        acc_ref[...] = part

    @pl.when(h > 0)
    def _():
        acc_ref[...] += part

    @pl.when(h == HEADS // PAIR - 1)
    def _():
        other_ref[...] = acc_ref[...].astype(BF16)


def attn_combine(core, masks, received, weight):
    return pl.pallas_call(
        attn_kernel,
        grid_spec=pltpu.PrefetchScalarGridSpec(
            num_scalar_prefetch=1,
            grid=(HEADS // PAIR,),
            in_specs=[
                pl.BlockSpec((PAIR, TOK, PER_HEAD), lambda h, core: (h, 0, 0)),
                VM,
                pl.BlockSpec((PAIR * DH, D // 2), lambda h, core: (h, 1 - core[0])),
            ],
            out_specs=[
                pl.BlockSpec((TOK, PAIR * DH), lambda h, core: (0, h)),
                pl.BlockSpec((TOK, D // 2), lambda h, core: (0, 0)),
            ],
            scratch_shapes=[pltpu.VMEM((TOK, D // 2), F32)],
        ),
        out_shape=[
            jax.ShapeDtypeStruct((TOK, HEADS * DH), BF16),
            jax.ShapeDtypeStruct((TOK, D // 2), BF16),
        ],
        name="attn_combine",
    )(core, masks, received, weight)


def grads_kernel(mask_hbm, in_hbm, dq_hbm, dk_hbm, dv_hbm, mask_ref, buf_ref, out_ref, in_sem, out_sem):
    outs = (dq_hbm, dk_hbm, dv_hbm)
    ins = []
    for h in range(HEADS):
        owners = pl.ds(h * OWNERS, OWNERS)
        a = pltpu.make_async_copy(mask_hbm.at[h], mask_ref.at[h], in_sem.at[h, 0])
        b = pltpu.make_async_copy(in_hbm.at[owners], buf_ref.at[owners], in_sem.at[h, 1])
        a.start()
        b.start()
        ins.append((a, b))
    sent = []
    for h in range(HEADS):
        for c in ins[h]:
            c.wait()
        owners = slice(h * OWNERS, (h + 1) * OWNERS)
        whole = jnp.concatenate([buf_ref[owners, j].reshape(PER_HEAD, DH) for j in range(3)], axis=1)
        got = matmul(mask_ref[h], whole).astype(BF16)
        for j in range(3):
            out_ref[j, :, h * DH : (h + 1) * DH] = got[:, j * DH : (j + 1) * DH]
        if h % PAIR == PAIR - 1:
            n = h // PAIR
            lanes = pl.ds(n * PAIR * DH, PAIR * DH)
            for j in range(3):
                c = pltpu.make_async_copy(out_ref.at[j, :, lanes], outs[j].at[:, lanes], out_sem.at[n, j])
                c.start()
                sent.append(c)
    for c in sent:
        c.wait()


def grads_combine(masks, received):
    return pl.pallas_call(
        grads_kernel,
        in_specs=[ANY] * 2,
        out_specs=[ANY] * 3,
        out_shape=[jax.ShapeDtypeStruct((TOK, HEADS * DH), BF16)] * 3,
        scratch_shapes=[
            pltpu.VMEM((HEADS, TOK, PER_HEAD), BF16),
            pltpu.VMEM((SEQ, 3, ROWS, DH), BF16),
            pltpu.VMEM((3, TOK, HEADS * DH), BF16),
            pltpu.SemaphoreType.DMA((HEADS, 2)),
            pltpu.SemaphoreType.DMA((HEADS // PAIR, 3)),
        ],
        name="grads_combine",
    )(masks, received)


def own_half_kernel(core_ref, attn_ref, w_ref, came_ref, out_ref):
    mine = matmul(attn_ref[...], w_ref[...])
    out_ref[...] = (mine + came_ref[...].astype(F32)).astype(BF16)


def own_half(core, attn, weight, came):
    width = 256
    steps = D // 2 // width
    return pl.pallas_call(
        own_half_kernel,
        grid_spec=pltpu.PrefetchScalarGridSpec(
            num_scalar_prefetch=1,
            grid=(steps,),
            in_specs=[
                pl.BlockSpec((TOK, HEADS * DH), lambda n, core: (0, 0)),
                pl.BlockSpec((HEADS * DH, width), lambda n, core: (0, core[0] * steps + n)),
                pl.BlockSpec((TOK, width), lambda n, core: (0, n)),
            ],
            out_specs=pl.BlockSpec((TOK, width), lambda n, core: (0, n)),
        ),
        out_shape=jax.ShapeDtypeStruct((TOK, D // 2), BF16),
        name="own_half",
    )(core, attn, weight, came)


def exchange(x):
    return lax.all_to_all(x, "seq", split_axis=0, concat_axis=0, tiled=True)


def in_vmem(x):
    return pltpu.with_memory_space_constraint(x, pltpu.MemorySpace.VMEM)


def body(query_rows, key_rows, value_rows, out_grad, cluster_ids, out_weight):
    idr = jnp.transpose(cluster_ids, (0, 2, 1))
    core = lax.axis_index("head").astype(jnp.int32).reshape(1)
    masks = token_masks(idr, cluster_ids)
    received = exchange(dispatch(core, idr, query_rows, key_rows, value_rows, out_grad, out_weight))
    attn_back = in_vmem(exchange(forward(received)))
    back = exchange(backward(received))
    attn, other = attn_combine(core, masks, attn_back, out_weight)
    came = lax.ppermute(other, "head", [(0, 1), (1, 0)])
    layer_out = own_half(core, attn, out_weight, came)
    dq, dk, dv = grads_combine(masks, back)
    return layer_out, dq, dk, dv


def solution(mesh):
    in_specs = (
        P("seq", "head"),
        P("seq", "head"),
        P("seq", "head"),
        P("seq", None),
        P("head", "seq", None),
        P("head", None),
    )
    out_specs = (P("seq", "head"), P("seq", "head"), P("seq", "head"), P("seq", "head"))
    return jax.shard_map(body, mesh=mesh, in_specs=in_specs, out_specs=out_specs, check_vma=False)
```
